512 devices in a mesh: pipe: 8 (over y_lo, core), tensor: 64 (over y_hi, x, z).
Axes of the slice: x: 4, y: 8 (y_hi: 2, y_lo: 4; y = y_hi * 4 + y_lo), z: 8, core: 2. Of those that a mesh axis runs over, the one named last changes fastest.
Arguments:
- output_gradient: bfloat16 [8, 64, 2, 64, 1024], P('pipe', 'tensor'), may hold values from -6 to 6
- forward_input: bfloat16 [8, 2, 512, 8192], P('pipe', None, None, 'tensor'), may hold values from -6 to 6
- saved_rank_outputs: bfloat16 [8, 2, 512, 64], P('pipe', None, 'tensor'), may hold values from -6 to 6
- projection_weight: bfloat16 [8, 64, 1024, 1024], P('pipe', 'tensor'), may hold values from -0.0625 to 0.0625
- adapter_down_maps: bfloat16 [8, 8, 64, 8192], P('pipe', None, None, 'tensor'), may hold values from -0.75 to 0.75
- adapter_up_maps: bfloat16 [8, 64, 8, 8, 1024], P('pipe', 'tensor'), may hold values from -0.0625 to 0.0625
- segment_adapter_class: int32 [8, 2, 4], P('pipe'), may hold values from 0 to 7
- live_segment_table: int32 [8, 2], P('pipe'), may hold values from 1 to 4, as said below
Outputs:
- grad_prev: bfloat16 [8, 2, 512, 8192], P('pipe', None, None, 'tensor')
- down_map_gradient: bfloat16 [8, 8, 64, 8192], P('pipe', None, None, 'tensor')
- up_map_gradient: bfloat16 [8, 64, 8, 8, 1024], P('pipe', 'tensor')
The draws below stay inside these ranges and needn't reach their ends.
Inputs may be any that keep to these rules, and one draw needn't show every extreme that they name: The first live_segment_table segments of a microbatch are live; some microbatch has all 4 live.
All inputs are finite; a program needn't handle non-finite values.
Results may differ from the reference program's by a relative error of at most 0.0049.
Values may be sent and summed in bfloat16 or wider, within the bound.
A program may use at most 64 MiB of HBM per device.

```python
import jax
import jax.numpy as jnp
from jax import lax

MODEL_WIDTH = 8192
ADAPTER_RANK = 64
SEG = 128
SEG_MB = 4
MICRO = 2
CLASS_ADAPTERS = 8
LOWER_GROUPS = 8
UPPER_GROUPS = 8
ROWS_MB = 512
ROWS = 1024
RELAY_SECTIONS = 8
N_TENSOR = 64


def draw_live_segment_table(key, part):
    first_key, second_key = jax.random.split(jax.random.fold_in(key, 17))
    values = jax.random.randint(first_key, (RELAY_SECTIONS * MICRO,), 1, SEG_MB + 1)
    picked = jax.random.randint(second_key, (), 0, RELAY_SECTIONS * MICRO)
    values = jnp.where(jnp.arange(RELAY_SECTIONS * MICRO) == picked, SEG_MB, values)
    return values.reshape(RELAY_SECTIONS, MICRO).astype(jnp.int32)


def touch_ends(values, own_key, low, largest):
    index_at = [jax.random.randint(jax.random.fold_in(own_key, axis), (), 0, length) for axis, length in enumerate(values.shape)]
    main_axis = values.shape.index(max(values.shape))
    neighbour = index_at[:main_axis] + [(index_at[main_axis] + 1) % values.shape[main_axis]] + index_at[main_axis + 1:]
    return values.at[tuple(index_at)].set(low).at[tuple(neighbour)].set(largest)


def levels(rng, extent, cuts, least, top_value):
    def one(position, shards_of):
        draws = jax.random.uniform(jax.random.fold_in(jax.random.fold_in(rng, 6), position), (shards_of,), jnp.float32, least / len(cuts), top_value / len(cuts))
        return jnp.repeat(jnp.exp(draws), extent[position] // shards_of).reshape((-1,) + (1,) * (len(extent) - position - 1))

    loudness = one(*cuts[0])
    for cut in cuts[1:]:
        loudness = loudness * one(*cut)
    return loudness


def scatter_about(key, extent, width, bound, shards=(), held_as=jnp.bfloat16):
    entries = jax.random.normal(key, extent, jnp.float32) * width
    if len(shards) > 0:
        entries = levels(key, extent, shards, -0.22, 0.18) * entries
    return jnp.clip(entries, min=-bound, max=bound).astype(held_as)


def setup_inputs(seed: int = 0) -> dict:
    streams_of = jax.random.split(jax.random.key(seed), 9)
    return {
        "output_gradient": scatter_about(streams_of[0], (RELAY_SECTIONS, N_TENSOR, MICRO, ROWS_MB // UPPER_GROUPS, MODEL_WIDTH // LOWER_GROUPS), 1.0, 6.0, ((0, 8), (1, 64))),
        "forward_input": scatter_about(streams_of[1], (RELAY_SECTIONS, MICRO, ROWS_MB, MODEL_WIDTH), 1.0, 6.0, ((0, 8), (3, 64))),
        "saved_rank_outputs": scatter_about(streams_of[2], (RELAY_SECTIONS, MICRO, ROWS_MB, ADAPTER_RANK), 1.0, 6.0, ((0, 8), (2, 64))),
        "projection_weight": scatter_about(streams_of[3], (RELAY_SECTIONS, N_TENSOR, MODEL_WIDTH // UPPER_GROUPS, MODEL_WIDTH // LOWER_GROUPS), MODEL_WIDTH ** -0.5, 0.0625, ((0, 8), (1, 64))),
        "adapter_down_maps": scatter_about(streams_of[4], (RELAY_SECTIONS, CLASS_ADAPTERS, ADAPTER_RANK, MODEL_WIDTH), ADAPTER_RANK ** -0.5, 0.75, ((0, 8), (3, 64))),
        "adapter_up_maps": scatter_about(streams_of[5], (RELAY_SECTIONS, N_TENSOR, CLASS_ADAPTERS, ADAPTER_RANK // UPPER_GROUPS, MODEL_WIDTH // LOWER_GROUPS), MODEL_WIDTH ** -0.5, 0.0625, ((0, 8), (1, 64))),
        "segment_adapter_class": touch_ends(jax.random.randint(streams_of[6], (RELAY_SECTIONS, MICRO, SEG_MB), 0, CLASS_ADAPTERS), jax.random.fold_in(streams_of[6], 1), 0, CLASS_ADAPTERS - 1).astype(jnp.int32),
        "live_segment_table": draw_live_segment_table(jax.random.fold_in(streams_of[8], 71), 0),
    }


def untile(tiles):
    arranged = tiles.reshape((UPPER_GROUPS, LOWER_GROUPS) + tiles.shape[1:])
    arranged = jnp.moveaxis(arranged, 0, -3)
    arranged = jnp.moveaxis(arranged, 0, -2)
    lead = arranged.shape[:-4]
    return arranged.reshape(lead + (UPPER_GROUPS * tiles.shape[-2], LOWER_GROUPS * tiles.shape[-1]))


def retile(whole):
    rank_part = ADAPTER_RANK // UPPER_GROUPS
    col_part = MODEL_WIDTH // LOWER_GROUPS
    arranged = whole.reshape(CLASS_ADAPTERS, UPPER_GROUPS, rank_part, LOWER_GROUPS, col_part)
    arranged = jnp.transpose(arranged, (1, 3, 0, 2, 4))
    return arranged.reshape(N_TENSOR, CLASS_ADAPTERS, rank_part, col_part)


def relay_section_backward(items):
    grad_tiles, inputs, hidden, weight_tiles, down_matrix, up_tiles, classes, live_count = items
    grads = untile(grad_tiles)
    weight = untile(weight_tiles)
    up_matrices = untile(up_tiles)
    seg_ids = jnp.arange(ROWS_MB, dtype=jnp.int32) // SEG
    keep_rows = seg_ids[None, :] < live_count[:, None]
    masked = jnp.where(keep_rows[:, :, None], grads, jnp.zeros_like(grads))
    class_indicator = (classes[:, :, None] == jnp.arange(CLASS_ADAPTERS, dtype=jnp.int32)[None, None, :]).astype(jnp.float32)
    highest_precision = lax.Precision.HIGHEST
    selected_up_matrix = jnp.einsum('pzw,wlq->pzlq', class_indicator, up_matrices.astype(jnp.float32), precision=highest_precision)
    selected_down_matrix = jnp.einsum('pzw,wlq->pzlq', class_indicator, down_matrix.astype(jnp.float32), precision=highest_precision)
    seg_grads = masked.reshape(MICRO, SEG_MB, SEG, MODEL_WIDTH).astype(jnp.float32)
    lowrank = jnp.einsum('mskd,msrd->mskr', seg_grads, selected_up_matrix, precision=highest_precision).astype(jnp.bfloat16)
    base_term = jnp.dot(masked.reshape(ROWS, MODEL_WIDTH), weight.T, preferred_element_type=jnp.float32)
    adapter = jnp.einsum('mskr,msrd->mskd', lowrank.astype(jnp.float32), selected_down_matrix, precision=highest_precision).reshape(ROWS, MODEL_WIDTH)
    input_gradient = (base_term + adapter).astype(jnp.bfloat16).reshape(MICRO, ROWS_MB, MODEL_WIDTH)
    seg_inputs = inputs.reshape(MICRO, SEG_MB, SEG, MODEL_WIDTH).astype(jnp.float32)
    seg_hidden = hidden.reshape(MICRO, SEG_MB, SEG, ADAPTER_RANK).astype(jnp.float32)
    segment_down_matrix = jnp.einsum('mskr,mskd->msrd', lowrank.astype(jnp.float32), seg_inputs, precision=highest_precision)
    segment_up_matrix = jnp.einsum('mskr,mskd->msrd', seg_hidden, seg_grads, precision=highest_precision)
    down_map_gradient = jnp.einsum('exk,exlq->klq', class_indicator, segment_down_matrix, precision=highest_precision).astype(jnp.bfloat16)
    up_map_gradient = jnp.einsum('exk,exlq->klq', class_indicator, segment_up_matrix, precision=highest_precision).astype(jnp.bfloat16)
    return input_gradient, down_map_gradient, retile(up_map_gradient)


def reference(output_gradient, forward_input, saved_rank_outputs, projection_weight, adapter_down_maps, adapter_up_maps, segment_adapter_class, live_segment_table):
    input_gradient, down_map_gradient, up_map_gradient = lax.map(relay_section_backward, (output_gradient, forward_input, saved_rank_outputs, projection_weight, adapter_down_maps, adapter_up_maps, segment_adapter_class, live_segment_table))
    grad_prev = jnp.roll(input_gradient, -1, axis=0)
    return grad_prev, down_map_gradient, up_map_gradient
```

```python
import jax
import jax.numpy as jnp
from jax import lax
from jax.experimental import pallas as pl
from jax.experimental.pallas import tpu as pltpu
from jax.sharding import PartitionSpec as P

MESH = pl.DeviceIdType.MESH
BF = jnp.bfloat16
F32 = jnp.float32
NX, NZ, NH, NP = 4, 8, 8, 8
ROWS = 64
LAG = 2
ORDER = (
    "O0", "O1", "L0", "R1", "L1", "R0", "X0", "X1",
    "Y0", "YL0", "YR0", "YX0", "Y1", "YL1", "YR1", "YX1",
)
SLOT = {name: i for i, name in enumerate(ORDER)}
N = len(ORDER)
SHIFT = {"O": 0, "L": 3, "R": 1, "X": 2, "Y": 0, "YL": 3, "YR": 1, "YX": 2}
ONWARD = {
    "L0": ((1, "X0"),),
    "R1": ((-1, "X1"),),
    "Y0": ((1, "YL0"), (-1, "YR0")),
    "Y1": ((1, "YL1"), (-1, "YR1")),
    "YL0": ((1, "YX0"),),
    "YR1": ((-1, "YX1"),),
}
EARLY = {6: ("Y0",), 11: ("Y1",)}
T_UP, T_SUM, T_SPREAD, T_RANK, T_DU, T_DA = 5, 8, 11, 17, 16, 18


def nt(a, b):
    return lax.dot_general(a, b, (((1,), (1,)), ((), ())), preferred_element_type=F32)


def nn(a, b):
    return lax.dot_general(a, b, (((1,), (0,)), ((), ())), preferred_element_type=F32)


def section(
    cls_ref, live_ref, g_ref, x_ref, hid_ref, w_ref, a_ref, u_ref,
    out_ref, da_ref, du_ref,
    gall, wv, pbuf, zs, zr, uf, us, ug, plb, plr, l2b, l2r, l3b, lfull, lt,
    hz, hkb, hk, xv, av, fin, dacc,
    loc, gss, grs, zss, zrs, uss, urs, l1s, l1r, l2s, l2rs, l3s, l3r, h1s, h1r, h2s, h2r, fs, fr,
):
    p = lax.axis_index("pipe")
    t = lax.axis_index("tensor")
    z = lax.rem(t, NZ)
    h = t // NZ
    x = lax.rem(h, NX)
    yh = h // NX

    def at_z(j):
        return (p, h * NZ + lax.rem(z + j + NZ, NZ))

    def at_h(j):
        return (p, lax.rem(h + j + NH, NH) * NZ + z)

    def at_x(j):
        return (p, (yh * NX + lax.rem(x + j + NX, NX)) * NZ + z)

    at_y = (p, ((1 - yh) * NX + x) * NZ + z)
    before = (lax.rem(p + NP - 1, NP), t)
    after = (lax.rem(p + 1, NP), t)

    def rows_of(name):
        shift = SHIFT[name[:-1]]
        there = 1 - yh if name[0] == "Y" else yh
        return there * NX + lax.rem(x + shift, NX), int(name[-1])

    bar = pltpu.get_barrier_semaphore()
    for j in range(1, NZ):
        pl.semaphore_signal(bar, inc=1, device_id=at_z(j), device_id_type=MESH)
    for j in range(1, NH):
        pl.semaphore_signal(bar, inc=1, device_id=at_h(j), device_id_type=MESH)
    pl.semaphore_signal(bar, inc=1, device_id=before, device_id_type=MESH)
    pl.semaphore_signal(bar, inc=1, device_id=after, device_id_type=MESH)

    loads = [
        pltpu.make_async_copy(g_ref.at[0], gall.at[0], loc.at[0]),
        pltpu.make_async_copy(g_ref.at[1], gall.at[1], loc.at[1]),
        pltpu.make_async_copy(w_ref, wv, loc.at[2]),
        pltpu.make_async_copy(x_ref, xv, loc.at[3]),
        pltpu.make_async_copy(a_ref, av, loc.at[4]),
    ]
    for load in loads:
        load.start()

    uf[...] = u_ref[...].astype(F32).reshape(uf.shape)
    for s in range(4):
        us[s] = jnp.concatenate([uf[cls_ref[s]], uf[cls_ref[4 + s]]], 0).astype(BF)
    ug[h] = us[h // 2]
    hz[z] = hid_ref[...]

    pl.semaphore_wait(bar, 16)

    sends = []

    def remote(src, dst, ssem, rsem, where):
        return pltpu.make_async_remote_copy(
            src_ref=src, dst_ref=dst, send_sem=ssem, recv_sem=rsem,
            device_id=where, device_id_type=MESH,
        )

    def send(*args):
        copy = remote(*args)
        copy.start()
        sends.append(copy)

    def g_send(src, k, where, name):
        send(src, gall.at[SLOT[name]], gss.at[k], grs.at[SLOT[name]], where)

    g_send(g_ref.at[0], 0, at_x(1), "L0")
    g_send(g_ref.at[1], 1, at_x(-1), "R1")
    g_send(g_ref.at[0], 2, at_y, "Y0")
    g_send(g_ref.at[1], 3, at_x(1), "L1")
    g_send(g_ref.at[0], 4, at_x(-1), "R0")
    for j in range(1, NH):
        there = lax.rem(h + j, NH)
        send(us.at[there // 2], ug.at[h], uss.at[j], urs.at[j], at_h(j))
    g_send(g_ref.at[1], 5, at_y, "Y1")
    for j in range(1, NZ):
        send(hid_ref, hz.at[z], h1s.at[j], h1r.at[j], at_z(j))
    count = [6]
    here = set()

    def arrive(name):
        if name in here:
            return
        here.add(name)
        slot = SLOT[name]
        if slot < 2:
            loads[slot].wait()
        else:
            remote(gall.at[slot], gall.at[slot], gss.at[0], grs.at[slot], at_y).wait_recv()
        for direction, name_there in ONWARD.get(name, ()):
            g_send(gall.at[slot], count[0], at_x(direction), name_there)
            count[0] += 1

    def hop(c, s):
        for d, sign in ((0, 1), (1, -1)):
            k = d * 4 + s - 1
            block = lax.rem(z + sign * (5 - s) + NZ, NZ)
            if s == 1:
                lo = 32 * d
                zs[c, k, 0:32, :] = pbuf[c, block, lo:lo + 32, :].astype(BF)
                src, dst = zs.at[c, k, 0:32], zr.at[c, k, 0:32]
            else:
                q = k - 1
                if s == 2:
                    got = zr.at[c, q, 0:32]
                else:
                    got = zr.at[c, q]
                remote(got, got, zss.at[c, q], zrs.at[c, q], at_z(sign)).wait_recv()
                if s == 2:
                    lo = 32 * d
                    other = 32 - lo
                    zs[c, k, lo:lo + 32, :] = (
                        pbuf[c, block, lo:lo + 32, :] + zr[c, q, 0:32, :].astype(F32)
                    ).astype(BF)
                    zs[c, k, other:other + 32, :] = pbuf[c, block, other:other + 32, :].astype(BF)
                else:
                    zs[c, k] = (pbuf[c, block] + zr[c, q].astype(F32)).astype(BF)
                src, dst = zs.at[c, k], zr.at[c, k]
            send(src, dst, zss.at[c, k], zrs.at[c, k], at_z(sign))

    lane = lax.broadcasted_iota(jnp.int32, (8, 128), 1)

    def of_block(b, table):
        return jnp.where(lane < ROWS, table(0, b // 2), table(1, b // 2))

    def class_or_none(m, s):
        return jnp.where(s < live_ref[m], cls_ref[m * 4 + s], -1)

    def alive(m, s):
        return jnp.where(s < live_ref[m], 1, 0)

    def emit(c):
        b, m = rows_of(ORDER[c])
        fin[c] = pbuf[c, z].astype(BF)
        send(
            fin.at[c], out_ref.at[m, pl.ds(pl.multiple_of(b * ROWS, ROWS), ROWS)],
            fs.at[c], fr.at[c], before,
        )

    adapters_in = [False]

    def finish(c):
        for q in (3, 7):
            remote(zr.at[c, q], zr.at[c, q], zss.at[c, q], zrs.at[c, q], at_z(1)).wait_recv()
        b, m = rows_of(ORDER[c])
        keep = jnp.zeros((ROWS, 128), jnp.int32) + alive(m, b // 2)
        total = pbuf[c, z] + zr[c, 3].astype(F32) + zr[c, 7].astype(F32)
        total = jnp.where(keep > 0, total, 0.0)
        if adapters_in[0]:
            total = total + lt[c]
        pbuf[c, z] = total
        if adapters_in[0]:
            emit(c)

    def up_rows():
        for j in range(1, NH):
            src = lax.rem(h - j + NH, NH)
            remote(ug.at[src], ug.at[src], uss.at[j], urs.at[j], at_h(j)).wait_recv()
        own = jnp.concatenate([gall[0], gall[1]], 0)
        both = nt(ug[...].reshape(128, 1024), own).reshape(8, 2, 8, 128)
        keep = of_block(h, alive)[None] > 0
        part = jnp.where(lane[None] < ROWS, both[:, 0], both[:, 1])
        plb[...] = jnp.where(keep, part, 0.0)
        plr[z] = plb[z]
        for j in range(1, NZ):
            there = lax.rem(z + j, NZ)
            send(plb.at[there], plr.at[z], l1s.at[j], l1r.at[j], at_z(j))

    def rank_sum():
        for j in range(1, NZ):
            src = lax.rem(z - j + NZ, NZ)
            remote(plr.at[src], plr.at[src], l1s.at[j], l1r.at[j], at_z(j)).wait_recv()
        total = jnp.sum(plr[...], 0).astype(BF).astype(F32)
        l2b[...] = total
        l2r[z] = total
        for j in range(1, NZ):
            send(l2b, l2r.at[z], l2s.at[j], l2rs.at[j], at_z(j))
        for j in range(1, NZ):
            src = lax.rem(z - j + NZ, NZ)
            remote(hz.at[src], hz.at[src], h1s.at[j], h1r.at[j], at_z(j)).wait_recv()
        hv = hz[...].astype(F32)
        hv = jnp.concatenate([hv[:, 0].reshape(64, 64), hv[:, 1].reshape(64, 64)], 0).astype(BF)
        r = lax.broadcasted_iota(jnp.int32, (64, 64), 0)
        c = lax.broadcasted_iota(jnp.int32, (64, 64), 1)
        hkb[...] = nt(jnp.where(r == c, 1.0, 0.0).astype(BF), hv).reshape(8, 8, 128)
        hk[h] = hkb[h]
        for j in range(1, NH):
            there = lax.rem(h + j, NH)
            send(hkb.at[there], hk.at[h], h2s.at[j], h2r.at[j], at_h(j))

    def rank_spread():
        for j in range(1, NZ):
            src = lax.rem(z - j + NZ, NZ)
            remote(l2r.at[src], l2r.at[src], l2s.at[j], l2rs.at[j], at_z(j)).wait_recv()
        mine = l2r[...].reshape(64, 128).astype(BF)
        l3b[...] = mine
        lfull[h] = mine
        for j in range(1, NH):
            send(l3b, lfull.at[h], l3s.at[j], l3r.at[j], at_h(j))

    def rank_here(done):
        for j in range(1, NH):
            src = lax.rem(h - j + NH, NH)
            remote(lfull.at[src], lfull.at[src], l3s.at[j], l3r.at[j], at_h(j)).wait_recv()
        loads[4].wait()
        r = lax.broadcasted_iota(jnp.int32, (128, 128), 0)
        c = lax.broadcasted_iota(jnp.int32, (128, 128), 1)
        eye = jnp.where(r == c, 1.0, 0.0).astype(BF)
        for name in ("O", "L", "R", "X", "Y", "YL", "YR", "YX"):
            b, _ = rows_of(name + "0")
            turned = nt(eye, lfull[b]).astype(BF)
            for m in range(2):
                slot = SLOT[name + str(m)]
                term = nn(turned[m * ROWS:(m + 1) * ROWS], av[cls_ref[m * 4 + b // 2]])
                if slot in done:
                    pbuf[slot, z] = pbuf[slot, z] + term
                else:
                    lt[slot] = term
        adapters_in[0] = True
        for slot in done:
            emit(slot)

    def up_gradient():
        for j in range(1, NH):
            src = lax.rem(h - j + NH, NH)
            remote(hk.at[src], hk.at[src], h2s.at[j], h2r.at[j], at_h(j)).wait_recv()
        number = lax.broadcasted_iota(jnp.int32, (8, 8, 128), 0)
        left, right = [], []
        for name in ("O", "L", "R", "X", "Y", "YL", "YR", "YX"):
            b, _ = rows_of(name + "0")
            chosen = of_block(b, class_or_none)[None]
            left.append(jnp.where(number == chosen, hk[b][None], 0.0).reshape(64, 128).astype(BF))
            right.append(gall[SLOT[name + "0"]])
            right.append(gall[SLOT[name + "1"]])
        du_ref[...] = nn(jnp.concatenate(left, 1), jnp.concatenate(right, 0)).astype(BF)

    def down_gradient():
        loads[3].wait()
        number = lax.broadcasted_iota(jnp.int32, (8, 64, 128), 0)
        for b in range(NH):
            wide = lax.broadcasted_iota(jnp.int32, (64, 128), 1)
            chosen = jnp.where(wide < ROWS, class_or_none(0, b // 2), class_or_none(1, b // 2))[None]
            left = jnp.where(number == chosen, lfull[b].astype(F32)[None], 0.0)
            left = left.reshape(512, 128).astype(BF)
            right = jnp.concatenate(
                [xv[0, b * ROWS:(b + 1) * ROWS], xv[1, b * ROWS:(b + 1) * ROWS]], 0
            )
            part = nn(left, right)
            if b == 0:
                dacc[...] = part
            elif b < NH - 1:
                dacc[...] += part
            else:
                da_ref[...] = (dacc[...] + part).astype(BF)

    loads[2].wait()
    done = []
    for step in range(N + 4 * LAG):
        if 0 <= step - 4 * LAG < N:
            finish(step - 4 * LAG)
            if not adapters_in[0]:
                done.append(step - 4 * LAG)
        for s in (4, 3, 2):
            if 0 <= step - LAG * (s - 1) < N:
                hop(step - LAG * (s - 1), s)
        for name in EARLY.get(step, ()):
            arrive(name)
        if step < N:
            arrive(ORDER[step])
            prod = nt(gall[step], wv[...])
            for j in range(NZ):
                pbuf[step, j] = prod[:, j * 128:(j + 1) * 128]
            hop(step, 1)
        if step == T_UP:
            up_rows()
        if step == T_SUM:
            rank_sum()
        if step == T_SPREAD:
            rank_spread()
        if step == T_RANK:
            rank_here(tuple(done))
        if step == T_DU:
            up_gradient()
        if step == T_DA:
            down_gradient()

    for c in range(N):
        b, m = rows_of(ORDER[c])
        dst = out_ref.at[m, pl.ds(pl.multiple_of(b * ROWS, ROWS), ROWS)]
        remote(fin.at[c], dst, fs.at[c], fr.at[c], before).wait_recv()
    for copy in sends:
        copy.wait_send()


def shards(
    output_gradient, forward_input, saved_rank_outputs, projection_weight,
    adapter_down_maps, adapter_up_maps, segment_adapter_class, live_segment_table,
):
    vm = pltpu.VMEM
    dma = pltpu.SemaphoreType.DMA
    smem = pl.BlockSpec(memory_space=pltpu.SMEM)
    vmem = pl.BlockSpec(memory_space=pltpu.VMEM)
    hbm = pl.BlockSpec(memory_space=pl.ANY)
    out, da, du = pl.pallas_call(
        section,
        name="section",
        out_shape=(
            jax.ShapeDtypeStruct((2, 512, 128), BF),
            jax.ShapeDtypeStruct((512, 128), BF),
            jax.ShapeDtypeStruct((64, 1024), BF),
        ),
        in_specs=[smem, smem, hbm, hbm, vmem, hbm, hbm, vmem],
        out_specs=(vmem, vmem, vmem),
        scratch_shapes=[
            vm((N, ROWS, 1024), BF), vm((1024, 1024), BF), vm((N, 8, ROWS, 128), F32),
            vm((N, 8, ROWS, 128), BF), vm((N, 8, ROWS, 128), BF),
            vm((8, 8, 1024), F32), vm((4, 16, 1024), BF), vm((8, 16, 1024), BF),
            vm((8, 8, 128), F32), vm((8, 8, 128), F32), vm((8, 128), F32), vm((8, 8, 128), F32),
            vm((64, 128), BF), vm((8, 64, 128), BF), vm((N, ROWS, 128), F32),
            vm((8, 2, 8, 64), BF), vm((8, 8, 128), F32), vm((8, 8, 128), F32),
            vm((2, 512, 128), BF), vm((8, 64, 128), BF), vm((N, ROWS, 128), BF), vm((512, 128), F32),
            dma((5,)), dma((16,)), dma((N,)), dma((N, 8)), dma((N, 8)),
            dma((8,)), dma((8,)), dma((8,)), dma((8,)), dma((8,)), dma((8,)),
            dma((8,)), dma((8,)), dma((8,)), dma((8,)), dma((8,)), dma((8,)), dma((N,)), dma((N,)),
        ],
        compiler_params=pltpu.CompilerParams(
            collective_id=0, has_side_effects=True, vmem_limit_bytes=48 * 1024 * 1024
        ),
    )(
        segment_adapter_class.reshape(8),
        live_segment_table.reshape(2),
        output_gradient.reshape(2, ROWS, 1024),
        forward_input.reshape(2, 512, 128),
        saved_rank_outputs.reshape(2, 8, 64),
        projection_weight.reshape(1024, 1024),
        adapter_down_maps.reshape(8, 64, 128),
        adapter_up_maps.reshape(64, 1024),
    )
    return (
        out.reshape(1, 2, 512, 128),
        da.reshape(1, 8, 64, 128),
        du.reshape(1, 1, 8, 8, 1024),
    )


def solution(mesh):
    in_specs = (
        P("pipe", "tensor", None, None, None),
        P("pipe", None, None, "tensor"),
        P("pipe", None, "tensor", None),
        P("pipe", "tensor", None, None),
        P("pipe", None, None, "tensor"),
        P("pipe", "tensor", None, None, None),
        P("pipe", None, None),
        P("pipe", None),
    )
    out_specs = (
        P("pipe", None, None, "tensor"),
        P("pipe", None, None, "tensor"),
        P("pipe", "tensor", None, None, None),
    )
    return jax.shard_map(shards, mesh=mesh, in_specs=in_specs, out_specs=out_specs, check_vma=False)
```

```python
import jax
import jax.numpy as jnp
from jax import lax
from jax.experimental import pallas as pl
from jax.experimental.pallas import tpu as pltpu
from jax.sharding import PartitionSpec as P

MESH = pl.DeviceIdType.MESH
BF = jnp.bfloat16
F32 = jnp.float32
NX, NZ, NH, NP = 4, 8, 8, 8
ROWS = 64
LAG = 4
ORDER = (
    "O0", "O1", "L0", "R0", "L1", "R1", "X0", "X1",
    "Y0", "YL0", "YR0", "Y1", "YX0", "YL1", "YR1", "YX1",
)
SLOT = {name: i for i, name in enumerate(ORDER)}
N = len(ORDER)
LAST = N - 1
SHIFT = {"O": 0, "L": 3, "R": 1, "X": 2, "Y": 0, "YL": 3, "YR": 1, "YX": 2}
ONWARD = {
    ("L0", 0): ((1, "X0"),),
    ("L1", 0): ((1, "X1"),),
    ("R0", 1): ((-1, "X0"),),
    ("R1", 1): ((-1, "X1"),),
    ("Y0", 0): ((1, "YL0"), (-1, "YR0")),
    ("Y0", 1): ((1, "YL0"), (-1, "YR0")),
    ("Y1", 0): ((1, "YL1"), (-1, "YR1")),
    ("Y1", 1): ((1, "YL1"), (-1, "YR1"), (2, "YX1")),
    ("YL0", 0): ((1, "YX0"),),
    ("YL1", 0): ((1, "YX1"),),
    ("YR0", 1): ((-1, "YX0"),),
}
EARLY = {
    7: (("Y0", 0),),
    9: (("YL0", 0), ("Y1", 0)),
    12: (("YL1", 0),),
}
EVENTS = {
    "up_relay": 3, "up_rows": 7, "rank_sum": 10, "rank_spread": 12, "rank_relay": 15,
    "up_gradient": 17, "rank_here": 23, "down_gradient": 26,
}


def nt(a, b):
    return lax.dot_general(a, b, (((1,), (1,)), ((), ())), preferred_element_type=F32)


def nn(a, b):
    return lax.dot_general(a, b, (((1,), (0,)), ((), ())), preferred_element_type=F32)


def section(
    cls_ref, live_ref, g_ref, x_ref, hid_ref, w_ref, a_ref, u_ref,
    out_ref, da_ref, du_ref,
    gall, wv, pbuf, zs, zr, uf, us, ug, plb, plr, l2b, l2r, l3b, lfull, lt,
    hz, hkb, hk, xv, av, fin, dacc, uv, hidv, uy, hy, zd, zdr,
    loc, gss, grs, zss, zrs, uss, urs, l1s, l1r, l2s, l2rs, l3s, l3r, h1s, h1r, h2s, h2r, fs, fr, zds, zdrs,
):
    p = lax.axis_index("pipe")
    t = lax.axis_index("tensor")
    z = lax.rem(t, NZ)
    h = t // NZ
    x = lax.rem(h, NX)
    yh = h // NX

    def at_z(j):
        return (p, h * NZ + lax.rem(z + j + NZ, NZ))

    def at_x(j):
        return (p, (yh * NX + lax.rem(x + j + NX, NX)) * NZ + z)

    hp = (1 - yh) * NX + x
    at_y = (p, hp * NZ + z)

    def from_x(j):
        return yh * NX + lax.rem(x - j + NX, NX), (1 - yh) * NX + lax.rem(x - j + NX, NX)

    before = (lax.rem(p + NP - 1, NP), t)
    after = (lax.rem(p + 1, NP), t)

    def rows_of(name):
        shift = SHIFT[name[:-1]]
        there = 1 - yh if name[0] == "Y" else yh
        return there * NX + lax.rem(x + shift, NX), int(name[-1])

    bar = pltpu.get_barrier_semaphore()
    for j in range(1, NZ):
        pl.semaphore_signal(bar, inc=1, device_id=at_z(j), device_id_type=MESH)
    for j in range(1, NX):
        pl.semaphore_signal(bar, inc=1, device_id=at_x(j), device_id_type=MESH)
    pl.semaphore_signal(bar, inc=1, device_id=at_y, device_id_type=MESH)
    pl.semaphore_signal(bar, inc=1, device_id=before, device_id_type=MESH)
    pl.semaphore_signal(bar, inc=1, device_id=after, device_id_type=MESH)

    loads = [
        pltpu.make_async_copy(u_ref, uv, loc.at[5]),
        pltpu.make_async_copy(hid_ref, hidv, loc.at[6]),
        pltpu.make_async_copy(g_ref.at[0], gall.at[0], loc.at[0]),
        pltpu.make_async_copy(g_ref.at[1], gall.at[1], loc.at[1]),
        pltpu.make_async_copy(w_ref, wv, loc.at[2]),
        pltpu.make_async_copy(x_ref, xv, loc.at[3]),
        pltpu.make_async_copy(a_ref, av, loc.at[4]),
    ]
    for load in loads:
        load.start()
    loads.pop(0).wait()
    loads.pop(0).wait()

    uf[...] = uv[...].astype(F32).reshape(uf.shape)
    for s in range(4):
        us[s] = jnp.concatenate([uf[cls_ref[0, 0, s]], uf[cls_ref[0, 1, s]]], 0).astype(BF)
    ug[h] = us[h // 2]
    hz[z] = hidv[...]

    pl.semaphore_wait(bar, 13)

    sends = []

    def remote(src, dst, ssem, rsem, where):
        return pltpu.make_async_remote_copy(
            src_ref=src, dst_ref=dst, send_sem=ssem, recv_sem=rsem,
            device_id=where, device_id_type=MESH,
        )

    def send(*args):
        copy = remote(*args)
        copy.start()
        sends.append(copy)

    count = [0]

    def g_send(src, where, name, half):
        slot = SLOT[name]
        dst = gall.at[slot, pl.ds(32 * half, 32)]
        send(src, dst, gss.at[count[0]], grs.at[slot, half], where)
        count[0] += 1

    def own(m, half):
        return g_ref.at[m, pl.ds(32 * half, 32)]

    send(us.at[pl.ds(2 * (1 - yh), 2)], uy, uss.at[0], urs.at[0], at_y)
    for m in range(2):
        for half in range(2):
            g_send(own(m, half), at_x(1), f"L{m}", half)
            g_send(own(m, half), at_x(-1), f"R{m}", half)
            g_send(own(m, half), at_y, f"Y{m}", half)
    for j in range(1, NZ):
        send(hidv, hz.at[z], h1s.at[j], h1r.at[j], at_z(j))
    for j in range(1, NX):
        there = lax.rem(x + j, NX)
        send(us.at[2 * yh + there // 2], ug.at[h], uss.at[j], urs.at[j], at_x(j))
    here = set()

    def arrive(name, halves=(0, 1)):
        slot = SLOT[name]
        for half in halves:
            if (name, half) in here:
                continue
            here.add((name, half))
            got = gall.at[slot, pl.ds(32 * half, 32)]
            if slot < 2:
                if half == 0:
                    loads[slot].wait()
            else:
                remote(got, got, gss.at[0], grs.at[slot, half], at_y).wait_recv()
            for direction, name_there in ONWARD.get((name, half), ()):
                g_send(got, at_x(direction), name_there, half)

    def direct():
        for j in (4, 3, 5, 2, 6, 1, 7):
            zd[j] = pbuf[LAST, lax.rem(z + j, NZ)].astype(BF)
            send(zd.at[j], zdr.at[z], zds.at[j], zdrs.at[j], at_z(j))

    def hop(c, s):
        for d, sign in ((0, 1), (1, -1)):
            k = d * 4 + s - 1
            block = lax.rem(z + sign * (5 - s) + NZ, NZ)
            if s == 1:
                lo = 32 * d
                zs[c, k, 0:32, :] = pbuf[c, block, lo:lo + 32, :].astype(BF)
                src, dst = zs.at[c, k, 0:32], zr.at[c, k, 0:32]
            else:
                q = k - 1
                if s == 2:
                    got = zr.at[c, q, 0:32]
                else:
                    got = zr.at[c, q]
                remote(got, got, zss.at[c, q], zrs.at[c, q], at_z(sign)).wait_recv()
                if s == 2:
                    lo = 32 * d
                    other = 32 - lo
                    zs[c, k, lo:lo + 32, :] = (
                        pbuf[c, block, lo:lo + 32, :] + zr[c, q, 0:32, :].astype(F32)
                    ).astype(BF)
                    zs[c, k, other:other + 32, :] = pbuf[c, block, other:other + 32, :].astype(BF)
                else:
                    zs[c, k] = (pbuf[c, block] + zr[c, q].astype(F32)).astype(BF)
                src, dst = zs.at[c, k], zr.at[c, k]
            send(src, dst, zss.at[c, k], zrs.at[c, k], at_z(sign))

    lane = lax.broadcasted_iota(jnp.int32, (8, 128), 1)

    def of_block(b, table):
        return jnp.where(lane < ROWS, table(0, b // 2), table(1, b // 2))

    def class_or_none(m, s):
        return jnp.where(s < live_ref[0, m], cls_ref[0, m, s], -1)

    def alive(m, s):
        return jnp.where(s < live_ref[0, m], 1, 0)

    def emit(c):
        b, m = rows_of(ORDER[c])
        fin[c] = pbuf[c, z].astype(BF)
        send(
            fin.at[c], out_ref.at[m, pl.ds(pl.multiple_of(b * ROWS, ROWS), ROWS)],
            fs.at[c], fr.at[c], before,
        )

    adapters_in = [False]

    def finish(c):
        if c == LAST:
            total = pbuf[c, z]
            for j in (1, 7, 2, 6, 3, 5, 4):
                src = lax.rem(z - j + NZ, NZ)
                remote(zdr.at[src], zdr.at[src], zds.at[j], zdrs.at[j], at_z(j)).wait_recv()
                total = total + zdr[src].astype(F32)
        else:
            for q in (3, 7):
                remote(zr.at[c, q], zr.at[c, q], zss.at[c, q], zrs.at[c, q], at_z(1)).wait_recv()
            total = pbuf[c, z] + zr[c, 3].astype(F32) + zr[c, 7].astype(F32)
        b, m = rows_of(ORDER[c])
        keep = jnp.zeros((ROWS, 128), jnp.int32) + alive(m, b // 2)
        total = jnp.where(keep > 0, total, 0.0)
        if adapters_in[0]:
            total = total + lt[c]
        pbuf[c, z] = total
        if adapters_in[0]:
            emit(c)

    def up_relay():
        remote(uy, uy, uss.at[0], urs.at[0], at_y).wait_recv()
        for j in range(1, NX):
            there = lax.rem(x + j, NX)
            send(uy.at[there // 2], ug.at[hp], uss.at[3 + j], urs.at[3 + j], at_x(j))
        ug[hp] = uy[x // 2]

    def up_rows():
        for j in range(1, NX):
            for k, src in zip((j, 3 + j), from_x(j)):
                remote(ug.at[src], ug.at[src], uss.at[k], urs.at[k], at_x(j)).wait_recv()
        own = jnp.concatenate([gall[0], gall[1]], 0)
        both = nt(ug[...].reshape(128, 1024), own).reshape(8, 2, 8, 128)
        keep = of_block(h, alive)[None] > 0
        part = jnp.where(lane[None] < ROWS, both[:, 0], both[:, 1])
        plb[...] = jnp.where(keep, part, 0.0)
        plr[z] = plb[z]
        for j in range(1, NZ):
            there = lax.rem(z + j, NZ)
            send(plb.at[there], plr.at[z], l1s.at[j], l1r.at[j], at_z(j))

    def rank_sum():
        for j in range(1, NZ):
            src = lax.rem(z - j + NZ, NZ)
            remote(plr.at[src], plr.at[src], l1s.at[j], l1r.at[j], at_z(j)).wait_recv()
        total = jnp.sum(plr[...], 0).astype(BF).astype(F32)
        l2b[...] = total
        l2r[z] = total
        for j in range(1, NZ):
            send(l2b, l2r.at[z], l2s.at[j], l2rs.at[j], at_z(j))
        for j in range(1, NZ):
            src = lax.rem(z - j + NZ, NZ)
            remote(hz.at[src], hz.at[src], h1s.at[j], h1r.at[j], at_z(j)).wait_recv()
        hv = hz[...].astype(F32)
        hv = jnp.concatenate([hv[:, 0].reshape(64, 64), hv[:, 1].reshape(64, 64)], 0).astype(BF)
        r = lax.broadcasted_iota(jnp.int32, (64, 64), 0)
        c = lax.broadcasted_iota(jnp.int32, (64, 64), 1)
        hkb[...] = nt(jnp.where(r == c, 1.0, 0.0).astype(BF), hv).reshape(8, 8, 128)
        hk[h] = hkb[h]
        send(hkb.at[pl.ds(NX * (1 - yh), NX)], hy, h2s.at[0], h2r.at[0], at_y)
        for j in range(1, NX):
            there = yh * NX + lax.rem(x + j, NX)
            send(hkb.at[there], hk.at[h], h2s.at[j], h2r.at[j], at_x(j))

    def rank_spread():
        for j in range(1, NZ):
            src = lax.rem(z - j + NZ, NZ)
            remote(l2r.at[src], l2r.at[src], l2s.at[j], l2rs.at[j], at_z(j)).wait_recv()
        mine = l2r[...].reshape(64, 128).astype(BF)
        l3b[...] = mine
        lfull[h] = mine
        send(l3b, lfull.at[h], l3s.at[0], l3r.at[0], at_y)
        for j in range(1, NX):
            send(l3b, lfull.at[h], l3s.at[j], l3r.at[j], at_x(j))

    def rank_relay():
        remote(lfull.at[hp], lfull.at[hp], l3s.at[0], l3r.at[0], at_y).wait_recv()
        for j in range(1, NX):
            send(lfull.at[hp], lfull.at[hp], l3s.at[3 + j], l3r.at[3 + j], at_x(j))
        remote(hy, hy, h2s.at[0], h2r.at[0], at_y).wait_recv()
        for j in range(1, NX):
            there = lax.rem(x + j, NX)
            send(hy.at[there], hk.at[hp], h2s.at[3 + j], h2r.at[3 + j], at_x(j))
        hk[hp] = hy[x]

    def rank_here(done):
        for j in range(1, NX):
            for k, src in zip((j, 3 + j), from_x(j)):
                remote(lfull.at[src], lfull.at[src], l3s.at[k], l3r.at[k], at_x(j)).wait_recv()
        loads[4].wait()
        r = lax.broadcasted_iota(jnp.int32, (128, 128), 0)
        c = lax.broadcasted_iota(jnp.int32, (128, 128), 1)
        eye = jnp.where(r == c, 1.0, 0.0).astype(BF)
        for name in ("O", "L", "R", "X", "Y", "YL", "YR", "YX"):
            b, _ = rows_of(name + "0")
            turned = nt(eye, lfull[b]).astype(BF)
            for m in range(2):
                slot = SLOT[name + str(m)]
                term = nn(turned[m * ROWS:(m + 1) * ROWS], av[cls_ref[0, m, b // 2]])
                if slot in done:
                    pbuf[slot, z] = pbuf[slot, z] + term
                else:
                    lt[slot] = term
        adapters_in[0] = True
        for slot in done:
            emit(slot)

    def up_gradient():
        for j in range(1, NX):
            for k, src in zip((j, 3 + j), from_x(j)):
                remote(hk.at[src], hk.at[src], h2s.at[k], h2r.at[k], at_x(j)).wait_recv()
        number = lax.broadcasted_iota(jnp.int32, (8, 8, 128), 0)
        left, right = [], []
        for name in ("O", "L", "R", "X", "Y", "YL", "YR", "YX"):
            b, _ = rows_of(name + "0")
            chosen = of_block(b, class_or_none)[None]
            left.append(jnp.where(number == chosen, hk[b][None], 0.0).reshape(64, 128).astype(BF))
            right.append(gall[SLOT[name + "0"]])
            right.append(gall[SLOT[name + "1"]])
        du_ref[...] = nn(jnp.concatenate(left, 1), jnp.concatenate(right, 0)).astype(BF)

    def down_gradient():
        loads[3].wait()
        number = lax.broadcasted_iota(jnp.int32, (8, 64, 128), 0)
        for b in range(NH):
            wide = lax.broadcasted_iota(jnp.int32, (64, 128), 1)
            chosen = jnp.where(wide < ROWS, class_or_none(0, b // 2), class_or_none(1, b // 2))[None]
            left = jnp.where(number == chosen, lfull[b].astype(F32)[None], 0.0)
            left = left.reshape(512, 128).astype(BF)
            right = jnp.concatenate(
                [xv[0, b * ROWS:(b + 1) * ROWS], xv[1, b * ROWS:(b + 1) * ROWS]], 0
            )
            part = nn(left, right)
            if b == 0:
                dacc[...] = part
            elif b < NH - 1:
                dacc[...] += part
            else:
                da_ref[...] = (dacc[...] + part).astype(BF)

    loads[2].wait()
    done = []
    for step in range(N + 4 * LAG):
        c = step - 4 * LAG
        if 0 <= c:
            finish(c)
            if not adapters_in[0]:
                done.append(c)
        for s in (4, 3, 2):
            if 0 <= step - LAG * (s - 1) < LAST:
                hop(step - LAG * (s - 1), s)
        for name, half in EARLY.get(step, ()):
            arrive(name, (half,))
        if step < N:
            arrive(ORDER[step])
            prod = nt(gall[step], wv[...])
            for j in range(NZ):
                pbuf[step, j] = prod[:, j * 128:(j + 1) * 128]
            if step == LAST:
                direct()
            else:
                hop(step, 1)
        if step == EVENTS["up_relay"]:
            up_relay()
        if step == EVENTS["up_rows"]:
            up_rows()
        if step == EVENTS["rank_sum"]:
            rank_sum()
        if step == EVENTS["rank_spread"]:
            rank_spread()
        if step == EVENTS["rank_relay"]:
            rank_relay()
        if step == EVENTS["rank_here"]:
            rank_here(tuple(done))
        if step == EVENTS["up_gradient"]:
            up_gradient()
        if step == EVENTS["down_gradient"]:
            down_gradient()

    for c in range(N):
        b, m = rows_of(ORDER[c])
        dst = out_ref.at[m, pl.ds(pl.multiple_of(b * ROWS, ROWS), ROWS)]
        remote(fin.at[c], dst, fs.at[c], fr.at[c], before).wait_recv()
    for copy in sends:
        copy.wait_send()


def shards(
    output_gradient, forward_input, saved_rank_outputs, projection_weight,
    adapter_down_maps, adapter_up_maps, segment_adapter_class, live_segment_table,
):
    vm = pltpu.VMEM
    dma = pltpu.SemaphoreType.DMA
    smem = pl.BlockSpec(memory_space=pltpu.SMEM)
    vmem = pl.BlockSpec(memory_space=pltpu.VMEM)
    hbm = pl.BlockSpec(memory_space=pl.ANY)
    out, da, du = pl.pallas_call(
        section,
        name="section",
        out_shape=(
            jax.ShapeDtypeStruct((2, 512, 128), BF),
            jax.ShapeDtypeStruct((512, 128), BF),
            jax.ShapeDtypeStruct((64, 1024), BF),
        ),
        in_specs=[smem, smem, hbm, hbm, hbm, hbm, hbm, hbm],
        out_specs=(vmem, vmem, vmem),
        scratch_shapes=[
            vm((N, ROWS, 1024), BF), vm((1024, 1024), BF), vm((N, 8, ROWS, 128), F32),
            vm((N, 8, ROWS, 128), BF), vm((N, 8, ROWS, 128), BF),
            vm((8, 8, 1024), F32), vm((4, 16, 1024), BF), vm((8, 16, 1024), BF),
            vm((8, 8, 128), F32), vm((8, 8, 128), F32), vm((8, 128), F32), vm((8, 8, 128), F32),
            vm((64, 128), BF), vm((8, 64, 128), BF), vm((N, ROWS, 128), F32),
            vm((8, 2, 8, 64), BF), vm((8, 8, 128), F32), vm((8, 8, 128), F32),
            vm((2, 512, 128), BF), vm((8, 64, 128), BF), vm((N, ROWS, 128), BF), vm((512, 128), F32),
            vm((64, 1024), BF), vm((2, 8, 64), BF),
            vm((2, 16, 1024), BF), vm((4, 8, 128), F32), vm((8, ROWS, 128), BF), vm((8, ROWS, 128), BF),
            dma((7,)), dma((32,)), dma((N, 2)), dma((N, 8)), dma((N, 8)),
            dma((8,)), dma((8,)), dma((8,)), dma((8,)), dma((8,)), dma((8,)),
            dma((8,)), dma((8,)), dma((8,)), dma((8,)), dma((8,)), dma((8,)), dma((N,)), dma((N,)), dma((8,)), dma((8,)),
        ],
        compiler_params=pltpu.CompilerParams(
            collective_id=0, has_side_effects=True, vmem_limit_bytes=67043328
        ),
    )(
        segment_adapter_class,
        live_segment_table,
        output_gradient.reshape(2, ROWS, 1024),
        forward_input.reshape(2, 512, 128),
        saved_rank_outputs.reshape(2, 8, 64),
        projection_weight.reshape(1024, 1024),
        adapter_down_maps.reshape(8, 64, 128),
        adapter_up_maps.reshape(64, 1024),
    )
    return (
        out.reshape(1, 2, 512, 128),
        da.reshape(1, 8, 64, 128),
        du.reshape(1, 1, 8, 8, 1024),
    )


def solution(mesh):
    in_specs = (
        P("pipe", "tensor", None, None, None),
        P("pipe", None, None, "tensor"),
        P("pipe", None, "tensor", None),
        P("pipe", "tensor", None, None),
        P("pipe", None, None, "tensor"),
        P("pipe", "tensor", None, None, None),
        P("pipe", None, None),
        P("pipe", None),
    )
    out_specs = (
        P("pipe", None, None, "tensor"),
        P("pipe", None, None, "tensor"),
        P("pipe", "tensor", None, None, None),
    )
    return jax.shard_map(shards, mesh=mesh, in_specs=in_specs, out_specs=out_specs, check_vma=False)
```

```python
import jax
import jax.numpy as jnp
from jax import lax
from jax.experimental import pallas as pl
from jax.experimental.pallas import tpu as pltpu
from jax.sharding import PartitionSpec as P

MESH = pl.DeviceIdType.MESH
BF = jnp.bfloat16
F32 = jnp.float32
NX, NZ, NH, NP = 4, 8, 8, 8
ROWS = 64
ORDER = (
    "O0", "O1", "L0", "R0", "L1", "R1", "X0", "X1",
    "Y0", "YL0", "YR0", "Y1", "YX0", "YL1", "YR1", "YX1",
)
SLOT = {name: i for i, name in enumerate(ORDER)}
N = len(ORDER)
TWO = (13, 14, 15)
SHIFT = {"O": 0, "L": 3, "R": 1, "X": 2, "Y": 0, "YL": 3, "YR": 1, "YX": 2}
ONWARD = {
    ("L0", 0): ((1, "X0"),),
    ("L1", 0): ((1, "X1"),),
    ("R0", 1): ((-1, "X0"),),
    ("R1", 1): ((-1, "X1"),),
    ("Y0", 0): ((1, "YL0"), (-1, "YR0")),
    ("Y0", 1): ((1, "YL0"), (-1, "YR0")),
    ("Y1", 0): ((1, "YL1"), (-1, "YR1")),
    ("Y1", 1): ((1, "YL1"), (-1, "YR1"), (2, "YX1")),
    ("YL0", 0): ((1, "YX0"),),
    ("YL1", 0): ((1, "YX1"),),
    ("YR0", 1): ((-1, "YX0"),),
}
PLAN = (
    ("mm", 0), ("mm", 1), ("hop", 0, 2, 0), ("hop", 0, 2, 1), ("fwd", "L0", 0), ("hop", 1, 2, 0),
    ("hop", 1, 2, 1), ("fwd", "R0", 1), ("mm", 2), ("mm", 3), ("fwd", "L1", 0), ("hop", 0, 3, 0),
    ("hop", 0, 3, 1), ("hop", 1, 3, 0), ("up_relay",), ("hop", 1, 3, 1), ("fwd", "R1", 1), ("mm", 4),
    ("mm", 5), ("hop", 2, 2, 0), ("hop", 2, 2, 1), ("hop", 3, 2, 0), ("hop", 3, 2, 1), ("hop", 0, 4, 0),
    ("fwd", "Y0", 0), ("hop", 0, 4, 1), ("hop", 1, 4, 0), ("hop", 1, 4, 1), ("mm", 6), ("hop", 4, 2, 0),
    ("hop", 4, 2, 1), ("hop", 5, 2, 0), ("hop", 5, 2, 1), ("hop", 2, 3, 0), ("hop", 2, 3, 1),
    ("fwd", "Y0", 1), ("mm", 8), ("hop", 3, 3, 0), ("hop", 3, 3, 1), ("fin", 0), ("up_rows",),
    ("fwd", "YL0", 0), ("fin", 1), ("hop", 6, 2, 0), ("hop", 6, 2, 1), ("mm", 7), ("fwd", "Y1", 0),
    ("hop", 4, 3, 0), ("hop", 2, 4, 0), ("hop", 2, 4, 1), ("hop", 4, 3, 1), ("hop", 5, 3, 0),
    ("hop", 5, 3, 1), ("hop", 8, 2, 0), ("hop", 8, 2, 1), ("hop", 3, 4, 0), ("hop", 3, 4, 1), ("mm", 9),
    ("fwd", "YR0", 1), ("mm", 10), ("fwd", "Y1", 1), ("mm", 11), ("fwd", "YL1", 0), ("hop", 6, 3, 0),
    ("hop", 6, 3, 1), ("hop", 7, 2, 0), ("hop", 7, 2, 1), ("hop", 4, 4, 0), ("hop", 4, 4, 1), ("fin", 2),
    ("hop", 5, 4, 0), ("hop", 5, 4, 1), ("mm", 12), ("rank_sum",), ("hop", 8, 3, 0), ("hop", 8, 3, 1),
    ("hop", 9, 2, 0), ("hop", 9, 2, 1), ("hop", 10, 2, 0), ("hop", 10, 2, 1), ("hop", 11, 2, 0),
    ("hop", 11, 2, 1), ("hop", 6, 4, 0), ("hop", 6, 4, 1), ("fin", 3), ("hop", 7, 3, 0), ("hop", 7, 3, 1),
    ("mm", 13), ("fin", 4), ("fin", 5), ("mm", 14), ("hop", 12, 2, 0), ("hop", 12, 2, 1), ("mm", 15),
    ("hop", 8, 4, 0), ("hop", 8, 4, 1), ("hop", 9, 3, 0), ("hop", 9, 3, 1), ("hop", 10, 3, 0),
    ("hop", 10, 3, 1), ("hop", 11, 3, 0), ("hop", 11, 3, 1), ("fin", 6), ("hop", 7, 4, 0), ("hop", 7, 4, 1),
    ("pair", 13, 0), ("pair", 13, 1), ("rank_relay",), ("pair", 14, 0), ("hop", 12, 3, 0), ("hop", 12, 3, 1),
    ("pair", 14, 1), ("pair", 15, 0), ("pair", 15, 1), ("fin", 8), ("hop", 9, 4, 0), ("hop", 9, 4, 1),
    ("hop", 10, 4, 0), ("hop", 10, 4, 1), ("hop", 11, 4, 0), ("hop", 11, 4, 1), ("fin", 7), ("hop", 12, 4, 1),
    ("rank_here",), ("hop", 12, 4, 0), ("fin", 13), ("down_gradient",), ("fin", 14), ("fin", 9),
    ("up_gradient",), ("fin", 10), ("fin", 11), ("fin", 15), ("fin", 12),
)


def nt(a, b):
    return lax.dot_general(a, b, (((1,), (1,)), ((), ())), preferred_element_type=F32)


def nn(a, b):
    return lax.dot_general(a, b, (((1,), (0,)), ((), ())), preferred_element_type=F32)


def section(
    cls_at, live_at, g_ref, x_ref, hid_ref, w_ref, a_ref, u_ref,
    out_ref, da_ref, du_ref,
    gall, wv, pbuf, zs, zr, uf, us, ug, plb, plr, l3b, lfull, lt,
    hz, hkb, hk, xv, av, fin, dacc, uv, hidv, uy, hy, cls_ref, live_ref,
    loc, gss, grs, zss, zrs, uss, urs, l1s, l1r, l3s, l3r, h1s, h1r, h2s, h2r, fs, fr,
):
    p = lax.axis_index("pipe")
    t = lax.axis_index("tensor")
    z = lax.rem(t, NZ)
    h = t // NZ
    x = lax.rem(h, NX)
    yh = h // NX

    def at_z(j):
        return (p, h * NZ + lax.rem(z + j + NZ, NZ))

    def at_x(j):
        return (p, (yh * NX + lax.rem(x + j + NX, NX)) * NZ + z)

    hp = (1 - yh) * NX + x
    at_y = (p, hp * NZ + z)

    def from_x(j):
        return yh * NX + lax.rem(x - j + NX, NX), (1 - yh) * NX + lax.rem(x - j + NX, NX)

    before = (lax.rem(p + NP - 1, NP), t)
    after = (lax.rem(p + 1, NP), t)

    def rows_of(name):
        shift = SHIFT[name[:-1]]
        there = 1 - yh if name[0] == "Y" else yh
        return there * NX + lax.rem(x + shift, NX), int(name[-1])

    bar = pltpu.get_barrier_semaphore()
    for j in range(1, NZ):
        pl.semaphore_signal(bar, inc=1, device_id=at_z(j), device_id_type=MESH)
    for j in range(1, NX):
        pl.semaphore_signal(bar, inc=1, device_id=at_x(j), device_id_type=MESH)
    pl.semaphore_signal(bar, inc=1, device_id=at_y, device_id_type=MESH)
    pl.semaphore_signal(bar, inc=1, device_id=before, device_id_type=MESH)
    pl.semaphore_signal(bar, inc=1, device_id=after, device_id_type=MESH)

    loads = [
        pltpu.make_async_copy(cls_at, cls_ref, loc.at[7]),
        pltpu.make_async_copy(live_at, live_ref, loc.at[8]),
        pltpu.make_async_copy(u_ref, uv, loc.at[5]),
        pltpu.make_async_copy(hid_ref, hidv, loc.at[6]),
        pltpu.make_async_copy(g_ref.at[0], gall.at[0], loc.at[0]),
        pltpu.make_async_copy(g_ref.at[1], gall.at[1], loc.at[1]),
        pltpu.make_async_copy(w_ref, wv, loc.at[2]),
        pltpu.make_async_copy(x_ref, xv, loc.at[3]),
        pltpu.make_async_copy(a_ref, av, loc.at[4]),
    ]
    for load in loads:
        load.start()
    for _ in range(4):
        loads.pop(0).wait()

    uf[...] = uv[...].astype(F32).reshape(uf.shape)
    for s in range(4):
        us[s] = jnp.concatenate([uf[cls_ref[0, 0, s]], uf[cls_ref[0, 1, s]]], 0).astype(BF)
    ug[h] = us[h // 2]
    hz[z] = hidv[...]

    pl.semaphore_wait(bar, 13)

    sends = []

    def remote(src, dst, ssem, rsem, where):
        return pltpu.make_async_remote_copy(
            src_ref=src, dst_ref=dst, send_sem=ssem, recv_sem=rsem,
            device_id=where, device_id_type=MESH,
        )

    def send(*args):
        copy = remote(*args)
        copy.start()
        sends.append(copy)

    count = [0]

    def g_send(src, where, name, half):
        slot = SLOT[name]
        dst = gall.at[slot, pl.ds(32 * half, 32)]
        send(src, dst, gss.at[count[0]], grs.at[slot, half], where)
        count[0] += 1

    def own(m, half):
        return g_ref.at[m, pl.ds(32 * half, 32)]

    send(us.at[pl.ds(2 * (1 - yh), 2)], uy, uss.at[0], urs.at[0], at_y)
    for m in range(2):
        for half in range(2):
            g_send(own(m, half), at_x(1), f"L{m}", half)
            g_send(own(m, half), at_x(-1), f"R{m}", half)
            g_send(own(m, half), at_y, f"Y{m}", half)
    for j in range(1, NZ):
        send(hidv, hz.at[z], h1s.at[j], h1r.at[j], at_z(j))
    for j in range(1, NX):
        there = lax.rem(x + j, NX)
        send(us.at[2 * yh + there // 2], ug.at[h], uss.at[j], urs.at[j], at_x(j))
    here = set()

    def arrive(name, halves=(0, 1)):
        slot = SLOT[name]
        for half in halves:
            if (name, half) in here:
                continue
            here.add((name, half))
            got = gall.at[slot, pl.ds(32 * half, 32)]
            if slot < 2:
                if half == 0:
                    loads[slot].wait()
            else:
                remote(got, got, gss.at[0], grs.at[slot, half], at_y).wait_recv()
            for direction, name_there in ONWARD.get((name, half), ()):
                g_send(got, at_x(direction), name_there, half)

    def got_z(c, q, sign, rows=ROWS):
        got = zr.at[c, q, pl.ds(0, rows)]
        remote(got, got, zss.at[c, q], zrs.at[c, q], at_z(sign)).wait_recv()
        return zr[c, q, 0:rows, :].astype(F32)

    def put_z(c, k, far, rows=ROWS):
        src, dst = zs.at[c, k, pl.ds(0, rows)], zr.at[c, k, pl.ds(0, rows)]
        send(src, dst, zss.at[c, k], zrs.at[c, k], at_z(far))

    def part(c, far):
        return pbuf.at[c, lax.rem(z + far + NZ, NZ)]

    def first(c):
        for d, sign in ((0, 1), (1, -1)):
            lo = 32 * d
            zs[c, 4 * d, 0:32, :] = part(c, 4)[lo:lo + 32, :].astype(BF)
            put_z(c, 4 * d, sign, 32)
            if c in TWO:
                zs[c, 4 * d + 1] = part(c, 2 * sign)[...].astype(BF)
                put_z(c, 4 * d + 1, sign)

    def with_half(c, k, d, sign):
        lo, other = 32 * d, 32 - 32 * d
        mine = part(c, 3 * sign)
        got = got_z(c, 4 * d, sign, 32)
        zs[c, k, lo:lo + 32, :] = (mine[lo:lo + 32, :] + got).astype(BF)
        zs[c, k, other:other + 32, :] = mine[other:other + 32, :].astype(BF)

    def hop(c, s, d):
        sign = 1 - 2 * d
        k = d * 4 + s - 1
        if s == 2:
            with_half(c, k, d, sign)
        else:
            zs[c, k] = (part(c, sign * (5 - s))[...] + got_z(c, k - 1, sign)).astype(BF)
        put_z(c, k, sign)

    def pair(c, d):
        sign = 1 - 2 * d
        with_half(c, 4 * d + 2, d, sign)
        put_z(c, 4 * d + 2, 3 * sign)
        zs[c, 4 * d + 3] = (part(c, sign)[...] + got_z(c, 4 * d + 1, sign)).astype(BF)
        put_z(c, 4 * d + 3, sign)

    lane = lax.broadcasted_iota(jnp.int32, (8, 128), 1)

    def of_block(b, table):
        return jnp.where(lane < ROWS, table(0, b // 2), table(1, b // 2))

    def class_or_none(m, s):
        return jnp.where(s < live_ref[0, m], cls_ref[0, m, s], -1)

    def alive(m, s):
        return jnp.where(s < live_ref[0, m], 1, 0)

    def emit(c):
        b, m = rows_of(ORDER[c])
        fin[c] = pbuf[c, z].astype(BF)
        send(
            fin.at[c], out_ref.at[m, pl.ds(pl.multiple_of(b * ROWS, ROWS), ROWS)],
            fs.at[c], fr.at[c], before,
        )

    adapters_in = [False]

    def finish(c):
        total = pbuf[c, z]
        for q in (2, 3, 6, 7) if c in TWO else (3, 7):
            total = total + got_z(c, q, 1)
        b, m = rows_of(ORDER[c])
        keep = jnp.zeros((ROWS, 128), jnp.int32) + alive(m, b // 2)
        total = jnp.where(keep > 0, total, 0.0)
        if adapters_in[0]:
            total = total + lt[c]
        pbuf[c, z] = total
        if adapters_in[0]:
            emit(c)

    def up_relay():
        remote(uy, uy, uss.at[0], urs.at[0], at_y).wait_recv()
        for j in range(1, NX):
            there = lax.rem(x + j, NX)
            send(uy.at[there // 2], ug.at[hp], uss.at[3 + j], urs.at[3 + j], at_x(j))
        ug[hp] = uy[x // 2]

    def up_rows():
        for j in range(1, NX):
            for k, src in zip((j, 3 + j), from_x(j)):
                remote(ug.at[src], ug.at[src], uss.at[k], urs.at[k], at_x(j)).wait_recv()
        own = jnp.concatenate([gall[0], gall[1]], 0)
        both = nt(ug[...].reshape(128, 1024), own).reshape(8, 2, 8, 128)
        keep = of_block(h, alive)[None] > 0
        half = jnp.where(lane[None] < ROWS, both[:, 0], both[:, 1])
        mine = jnp.where(keep, half, 0.0).reshape(64, 128).astype(BF)
        plb[...] = mine
        plr[z] = mine
        for j in (4, 3, 5, 2, 6, 1, 7):
            send(plb, plr.at[z], l1s.at[j], l1r.at[j], at_z(j))

    def rank_sum():
        for j in range(1, NZ):
            src = lax.rem(z - j + NZ, NZ)
            remote(plr.at[src], plr.at[src], l1s.at[j], l1r.at[j], at_z(j)).wait_recv()
        mine = jnp.sum(plr[...].astype(F32), 0).astype(BF)
        l3b[...] = mine
        lfull[h] = mine
        send(l3b, lfull.at[h], l3s.at[0], l3r.at[0], at_y)
        for j in range(1, NX):
            send(l3b, lfull.at[h], l3s.at[j], l3r.at[j], at_x(j))
        for j in range(1, NZ):
            src = lax.rem(z - j + NZ, NZ)
            remote(hz.at[src], hz.at[src], h1s.at[j], h1r.at[j], at_z(j)).wait_recv()
        hv = hz[...].astype(F32)
        hv = jnp.concatenate([hv[:, 0].reshape(64, 64), hv[:, 1].reshape(64, 64)], 0).astype(BF)
        r = lax.broadcasted_iota(jnp.int32, (64, 64), 0)
        c = lax.broadcasted_iota(jnp.int32, (64, 64), 1)
        hkb[...] = nt(jnp.where(r == c, 1.0, 0.0).astype(BF), hv).reshape(8, 8, 128)
        hk[h] = hkb[h]
        send(hkb.at[pl.ds(NX * (1 - yh), NX)], hy, h2s.at[0], h2r.at[0], at_y)
        for j in range(1, NX):
            there = yh * NX + lax.rem(x + j, NX)
            send(hkb.at[there], hk.at[h], h2s.at[j], h2r.at[j], at_x(j))

    def rank_relay():
        remote(lfull.at[hp], lfull.at[hp], l3s.at[0], l3r.at[0], at_y).wait_recv()
        for j in range(1, NX):
            send(lfull.at[hp], lfull.at[hp], l3s.at[3 + j], l3r.at[3 + j], at_x(j))
        remote(hy, hy, h2s.at[0], h2r.at[0], at_y).wait_recv()
        for j in range(1, NX):
            there = lax.rem(x + j, NX)
            send(hy.at[there], hk.at[hp], h2s.at[3 + j], h2r.at[3 + j], at_x(j))
        hk[hp] = hy[x]

    def rank_here(done):
        for j in range(1, NX):
            for k, src in zip((j, 3 + j), from_x(j)):
                remote(lfull.at[src], lfull.at[src], l3s.at[k], l3r.at[k], at_x(j)).wait_recv()
        loads[4].wait()
        r = lax.broadcasted_iota(jnp.int32, (128, 128), 0)
        c = lax.broadcasted_iota(jnp.int32, (128, 128), 1)
        eye = jnp.where(r == c, 1.0, 0.0).astype(BF)
        for name in ("O", "L", "R", "X", "Y", "YL", "YR", "YX"):
            b, _ = rows_of(name + "0")
            turned = nt(eye, lfull[b]).astype(BF)
            for m in range(2):
                slot = SLOT[name + str(m)]
                term = nn(turned[m * ROWS:(m + 1) * ROWS], av[cls_ref[0, m, b // 2]])
                if slot in done:
                    pbuf[slot, z] = pbuf[slot, z] + term
                else:
                    lt[slot] = term
        adapters_in[0] = True
        for slot in done:
            emit(slot)

    def up_gradient():
        for j in range(1, NX):
            for k, src in zip((j, 3 + j), from_x(j)):
                remote(hk.at[src], hk.at[src], h2s.at[k], h2r.at[k], at_x(j)).wait_recv()
        number = lax.broadcasted_iota(jnp.int32, (8, 8, 128), 0)
        left, right = [], []
        for name in ("O", "L", "R", "X", "Y", "YL", "YR", "YX"):
            b, _ = rows_of(name + "0")
            chosen = of_block(b, class_or_none)[None]
            left.append(jnp.where(number == chosen, hk[b][None], 0.0).reshape(64, 128).astype(BF))
            right.append(gall[SLOT[name + "0"]])
            right.append(gall[SLOT[name + "1"]])
        du_ref[...] = nn(jnp.concatenate(left, 1), jnp.concatenate(right, 0)).astype(BF)

    def down_gradient():
        loads[3].wait()
        number = lax.broadcasted_iota(jnp.int32, (8, 64, 128), 0)
        for b in range(NH):
            wide = lax.broadcasted_iota(jnp.int32, (64, 128), 1)
            chosen = jnp.where(wide < ROWS, class_or_none(0, b // 2), class_or_none(1, b // 2))[None]
            left = jnp.where(number == chosen, lfull[b].astype(F32)[None], 0.0)
            left = left.reshape(512, 128).astype(BF)
            right = jnp.concatenate(
                [xv[0, b * ROWS:(b + 1) * ROWS], xv[1, b * ROWS:(b + 1) * ROWS]], 0
            )
            term = nn(left, right)
            if b == 0:
                dacc[...] = term
            elif b < NH - 1:
                dacc[...] += term
            else:
                da_ref[...] = (dacc[...] + term).astype(BF)

    loads[2].wait()
    done = []

    def multiply(c):
        arrive(ORDER[c])
        prod = nt(gall[c], wv[...])
        for j in range(NZ):
            pbuf[c, j] = prod[:, j * 128:(j + 1) * 128]
        first(c)

    def close(c):
        finish(c)
        if not adapters_in[0]:
            done.append(c)

    does = {
        "fwd": lambda name, half: arrive(name, (half,)),
        "mm": multiply, "hop": hop, "pair": pair, "fin": close,
        "up_relay": up_relay, "up_rows": up_rows, "rank_sum": rank_sum,
        "rank_relay": rank_relay, "rank_here": lambda: rank_here(tuple(done)),
        "up_gradient": up_gradient, "down_gradient": down_gradient,
    }
    for what, *which in PLAN:
        does[what](*which)

    for c in range(N):
        b, m = rows_of(ORDER[c])
        dst = out_ref.at[m, pl.ds(pl.multiple_of(b * ROWS, ROWS), ROWS)]
        remote(fin.at[c], dst, fs.at[c], fr.at[c], before).wait_recv()
    for copy in sends:
        copy.wait_send()


def hand_out(out, da, du, out_to, da_to, du_to):
    out_to[...] = out[...]
    da_to[...] = da[...]
    du_to[...] = du[...]


def shards(
    output_gradient, forward_input, saved_rank_outputs, projection_weight,
    adapter_down_maps, adapter_up_maps, segment_adapter_class, live_segment_table,
):
    vm = pltpu.VMEM
    dma = pltpu.SemaphoreType.DMA
    vmem = pl.BlockSpec(memory_space=pltpu.VMEM)
    hbm = pl.BlockSpec(memory_space=pl.ANY)
    shapes = (
        jax.ShapeDtypeStruct((2, 512, 128), BF),
        jax.ShapeDtypeStruct((512, 128), BF),
        jax.ShapeDtypeStruct((64, 1024), BF),
    )
    outs = pl.pallas_call(
        section,
        name="section",
        out_shape=shapes,
        in_specs=[hbm, hbm, hbm, hbm, hbm, hbm, hbm, hbm],
        out_specs=(vmem, vmem, vmem),
        scratch_shapes=[
            vm((N, ROWS, 1024), BF), vm((1024, 1024), BF), vm((N, 8, ROWS, 128), F32),
            vm((N, 8, ROWS, 128), BF), vm((N, 8, ROWS, 128), BF),
            vm((8, 8, 1024), F32), vm((4, 16, 1024), BF), vm((8, 16, 1024), BF),
            vm((64, 128), BF), vm((8, 64, 128), BF), vm((64, 128), BF), vm((8, 64, 128), BF),
            vm((N, ROWS, 128), F32),
            vm((8, 2, 8, 64), BF), vm((8, 8, 128), F32), vm((8, 8, 128), F32),
            vm((2, 512, 128), BF), vm((8, 64, 128), BF), vm((N, ROWS, 128), BF), vm((512, 128), F32),
            vm((64, 1024), BF), vm((2, 8, 64), BF),
            vm((2, 16, 1024), BF), vm((4, 8, 128), F32),
            pltpu.SMEM((1, 2, 4), jnp.int32), pltpu.SMEM((1, 2), jnp.int32),
            dma((9,)), dma((32,)), dma((N, 2)), dma((N, 8)), dma((N, 8)),
            dma((8,)), dma((8,)), dma((8,)), dma((8,)), dma((8,)), dma((8,)),
            dma((8,)), dma((8,)), dma((8,)), dma((8,)), dma((N,)), dma((N,)),
        ],
        compiler_params=pltpu.CompilerParams(
            collective_id=0, has_side_effects=True, vmem_limit_bytes=40 * 1024 * 1024
        ),
    )(
        pltpu.with_memory_space_constraint(segment_adapter_class, pltpu.HBM),
        pltpu.with_memory_space_constraint(live_segment_table, pltpu.HBM),
        pltpu.with_memory_space_constraint(output_gradient.reshape(2, ROWS, 1024), pltpu.HBM),
        pltpu.with_memory_space_constraint(forward_input.reshape(2, 512, 128), pltpu.HBM),
        pltpu.with_memory_space_constraint(saved_rank_outputs.reshape(2, 8, 64), pltpu.HBM),
        pltpu.with_memory_space_constraint(projection_weight.reshape(1024, 1024), pltpu.HBM),
        pltpu.with_memory_space_constraint(adapter_down_maps.reshape(8, 64, 128), pltpu.HBM),
        pltpu.with_memory_space_constraint(adapter_up_maps.reshape(64, 1024), pltpu.HBM),
    )
    out, da, du = pl.pallas_call(
        hand_out,
        name="hand_out",
        out_shape=shapes,
        in_specs=[vmem] * 3,
        out_specs=(vmem,) * 3,
    )(*[pltpu.with_memory_space_constraint(o, pltpu.VMEM) for o in outs])
    return (
        out.reshape(1, 2, 512, 128),
        da.reshape(1, 8, 64, 128),
        du.reshape(1, 1, 8, 8, 1024),
    )


def solution(mesh):
    in_specs = (
        P("pipe", "tensor", None, None, None),
        P("pipe", None, None, "tensor"),
        P("pipe", None, "tensor", None),
        P("pipe", "tensor", None, None),
        P("pipe", None, None, "tensor"),
        P("pipe", "tensor", None, None, None),
        P("pipe", None, None),
        P("pipe", None),
    )
    out_specs = (
        P("pipe", None, None, "tensor"),
        P("pipe", None, None, "tensor"),
        P("pipe", "tensor", None, None, None),
    )
    return jax.shard_map(shards, mesh=mesh, in_specs=in_specs, out_specs=out_specs, check_vma=False)
```

```python
import jax
import jax.numpy as jnp
from jax import lax
from jax.experimental import pallas as pl
from jax.experimental.pallas import tpu as pltpu
from jax.sharding import PartitionSpec as P

MESH = pl.DeviceIdType.MESH
BF = jnp.bfloat16
F32 = jnp.float32
NX, NZ, NH, NP = 4, 8, 8, 8
ROWS = 64
ORDER = (
    "O0", "O1", "L0", "R0", "L1", "R1", "X0", "X1",
    "Y0", "YL0", "YR0", "Y1", "YX0", "YL1", "YR1", "YX1",
)
SLOT = {name: i for i, name in enumerate(ORDER)}
N = len(ORDER)
TWO = (7, 13, 14, 15)
SHIFT = {"O": 0, "L": 3, "R": 1, "X": 2, "Y": 0, "YL": 3, "YR": 1, "YX": 2}
ONWARD = {
    ("L0", 0): ((1, "X0"),),
    ("L1", 0): ((1, "X1"),),
    ("R0", 1): ((-1, "X0"),),
    ("R1", 1): ((-1, "X1"),),
    ("Y0", 0): ((1, "YL0"), (-1, "YR0")),
    ("Y0", 1): ((1, "YL0"), (-1, "YR0"), (2, "YX0")),
    ("Y1", 0): ((1, "YL1"), (-1, "YR1")),
    ("Y1", 1): ((1, "YL1"), (-1, "YR1"), (2, "YX1")),
    ("YL0", 0): ((1, "YX0"),),
    ("YL1", 0): ((1, "YX1"),),
}
PLAN = (
    ("mm", 0, 1), ("hop", 0, 2, 0), ("hop", 0, 2, 1), ("hop", 1, 2, 1), ("hop", 1, 2, 0), ("fwd", "L0", 0),
    ("fwd", "R0", 1), ("mm", 2, 3), ("hop", 0, 3, 0), ("hop", 0, 3, 1), ("fwd", "L1", 0), ("hop", 1, 3, 0),
    ("hop", 1, 3, 1), ("up_relay",), ("fwd", "R1", 1), ("mm", 4, 5), ("hop", 2, 2, 0), ("hop", 2, 2, 1),
    ("hop", 3, 2, 1), ("hop", 3, 2, 0), ("hop", 0, 4, 0), ("hop", 0, 4, 1), ("hop", 1, 4, 0),
    ("hop", 1, 4, 1), ("fwd", "Y0", 0), ("mm", 6), ("hop", 4, 2, 0), ("hop", 5, 2, 0), ("hop", 2, 3, 0),
    ("hop", 5, 2, 1), ("hop", 2, 3, 1), ("hop", 3, 3, 0), ("hop", 3, 3, 1), ("hop", 4, 2, 1),
    ("fwd", "Y0", 1), ("mm", 8), ("fin", 1), ("fin", 0), ("up_rows",), ("fwd", "YL0", 0), ("hop", 6, 2, 0),
    ("hop", 6, 2, 1), ("hop", 4, 3, 0), ("hop", 5, 3, 1), ("hop", 5, 3, 0), ("fwd", "Y1", 0), ("mm", 7),
    ("hop", 2, 4, 1), ("hop", 8, 2, 0), ("hop", 4, 3, 1), ("hop", 3, 4, 0), ("hop", 2, 4, 0),
    ("hop", 3, 4, 1), ("hop", 8, 2, 1), ("mm", 9, 10), ("fwd", "Y1", 1), ("mm", 11), ("mm", 12),
    ("hop", 6, 3, 0), ("hop", 5, 4, 1), ("hop", 4, 4, 0), ("hop", 6, 3, 1), ("hop", 5, 4, 0), ("pair", 7, 1),
    ("fwd", "YL1", 0), ("pair", 7, 0), ("hop", 8, 3, 0), ("hop", 4, 4, 1), ("rank_sum",), ("fin", 2),
    ("hop", 9, 2, 0), ("hop", 10, 2, 1), ("hop", 10, 2, 0), ("hop", 9, 2, 1), ("hop", 8, 3, 1),
    ("hop", 12, 2, 0), ("hop", 12, 2, 1), ("hop", 11, 2, 0), ("hop", 6, 4, 0), ("hop", 11, 2, 1),
    ("mm", 13, 14), ("hop", 6, 4, 1), ("fin", 5), ("fin", 3), ("mm", 15), ("hop", 8, 4, 0), ("hop", 10, 3, 1),
    ("fin", 4), ("hop", 9, 3, 1), ("hop", 9, 3, 0), ("hop", 10, 3, 0), ("hop", 8, 4, 1), ("hop", 12, 3, 0),
    ("hop", 12, 3, 1), ("fin", 7), ("hop", 11, 3, 0), ("hop", 11, 3, 1), ("rank_relay",), ("pair", 13, 1),
    ("pair", 13, 0), ("pair", 14, 1), ("pair", 14, 0), ("fin", 6), ("pair", 15, 0), ("pair", 15, 1),
    ("hop", 10, 4, 1), ("hop", 9, 4, 0), ("hop", 9, 4, 1), ("hop", 10, 4, 0), ("fin", 8), ("hop", 12, 4, 0),
    ("hop", 12, 4, 1), ("hop", 11, 4, 0), ("hop", 11, 4, 1), ("rank_here",), ("down_gradient",), ("fin", 13),
    ("up_gradient",), ("fin", 14), ("fin", 9), ("fin", 10), ("fin", 12), ("fin", 15), ("fin", 11),
)


def nt(a, b):
    return lax.dot_general(a, b, (((1,), (1,)), ((), ())), preferred_element_type=F32)


def nn(a, b):
    return lax.dot_general(a, b, (((1,), (0,)), ((), ())), preferred_element_type=F32)


def section(
    cls_at, live_at, g_ref, x_ref, hid_ref, w_ref, a_ref, u_ref,
    out_ref, da_ref, du_ref,
    gall, wv, wt, pbuf, zs, zr, uf, us, ug, plb, plr, l3b, lfull, lt,
    hz, hkb, hk, xv, av, fin, dacc, uv, hidv, uy, hy, cls_ref, live_ref,
    loc, gss, grs, zss, zrs, uss, urs, l1s, l1r, l3s, l3r, h1s, h1r, h2s, h2r, fs, fr,
):
    p = lax.axis_index("pipe")
    t = lax.axis_index("tensor")
    z = lax.rem(t, NZ)
    h = t // NZ
    x = lax.rem(h, NX)
    yh = h // NX

    def at_z(j):
        return (p, h * NZ + lax.rem(z + j + NZ, NZ))

    def at_x(j):
        return (p, (yh * NX + lax.rem(x + j + NX, NX)) * NZ + z)

    hp = (1 - yh) * NX + x
    at_y = (p, hp * NZ + z)

    def from_x(j):
        return yh * NX + lax.rem(x - j + NX, NX), (1 - yh) * NX + lax.rem(x - j + NX, NX)

    before = (lax.rem(p + NP - 1, NP), t)
    after = (lax.rem(p + 1, NP), t)

    def rows_of(name):
        shift = SHIFT[name[:-1]]
        there = 1 - yh if name[0] == "Y" else yh
        return there * NX + lax.rem(x + shift, NX), int(name[-1])

    bar = pltpu.get_barrier_semaphore()
    for j in range(1, NZ):
        pl.semaphore_signal(bar, inc=1, device_id=at_z(j), device_id_type=MESH)
    for j in range(1, NX):
        pl.semaphore_signal(bar, inc=1, device_id=at_x(j), device_id_type=MESH)
    pl.semaphore_signal(bar, inc=1, device_id=at_y, device_id_type=MESH)
    pl.semaphore_signal(bar, inc=1, device_id=before, device_id_type=MESH)
    pl.semaphore_signal(bar, inc=1, device_id=after, device_id_type=MESH)

    loads = [
        pltpu.make_async_copy(cls_at, cls_ref, loc.at[7]),
        pltpu.make_async_copy(live_at, live_ref, loc.at[8]),
        pltpu.make_async_copy(u_ref, uv, loc.at[5]),
        pltpu.make_async_copy(hid_ref, hidv, loc.at[6]),
        pltpu.make_async_copy(g_ref.at[0], gall.at[0], loc.at[0]),
        pltpu.make_async_copy(g_ref.at[1], gall.at[1], loc.at[1]),
        pltpu.make_async_copy(w_ref, wv, loc.at[2]),
        pltpu.make_async_copy(x_ref, xv, loc.at[3]),
        pltpu.make_async_copy(a_ref, av, loc.at[4]),
    ]
    for load in loads:
        load.start()
    for _ in range(4):
        loads.pop(0).wait()

    uf[...] = uv[...].astype(F32).reshape(uf.shape)
    for s in range(4):
        us[s] = jnp.concatenate([uf[cls_ref[0, 0, s]], uf[cls_ref[0, 1, s]]], 0).astype(BF)
    ug[h] = us[h // 2]
    hz[z] = hidv[...]

    loads[2].wait()
    wt[...] = wv[...].T
    pl.semaphore_wait(bar, 13)

    sends = []

    def remote(src, dst, ssem, rsem, where):
        return pltpu.make_async_remote_copy(
            src_ref=src, dst_ref=dst, send_sem=ssem, recv_sem=rsem,
            device_id=where, device_id_type=MESH,
        )

    def send(*args):
        copy = remote(*args)
        copy.start()
        sends.append(copy)

    count = [0]

    def g_send(src, where, name, half):
        slot = SLOT[name]
        dst = gall.at[slot, pl.ds(32 * half, 32)]
        send(src, dst, gss.at[count[0]], grs.at[slot, half], where)
        count[0] += 1

    def own(m, half):
        return g_ref.at[m, pl.ds(32 * half, 32)]

    send(us.at[pl.ds(2 * (1 - yh), 2)], uy, uss.at[0], urs.at[0], at_y)
    for m in range(2):
        for half in range(2):
            g_send(own(m, half), at_x(1), f"L{m}", half)
            g_send(own(m, half), at_x(-1), f"R{m}", half)
            g_send(own(m, half), at_y, f"Y{m}", half)
    for j in range(1, NZ):
        send(hidv, hz.at[z], h1s.at[j], h1r.at[j], at_z(j))
    for j in range(1, NX):
        there = lax.rem(x + j, NX)
        send(us.at[2 * yh + there // 2], ug.at[h], uss.at[j], urs.at[j], at_x(j))
    here = set()

    def arrive(name, halves=(0, 1)):
        slot = SLOT[name]
        for half in halves:
            if (name, half) in here:
                continue
            here.add((name, half))
            got = gall.at[slot, pl.ds(32 * half, 32)]
            if slot < 2:
                if half == 0:
                    loads[slot].wait()
            else:
                remote(got, got, gss.at[0], grs.at[slot, half], at_y).wait_recv()
            for direction, name_there in ONWARD.get((name, half), ()):
                g_send(got, at_x(direction), name_there, half)

    def got_z(c, q, sign, rows=ROWS):
        got = zr.at[c, q, pl.ds(0, rows)]
        remote(got, got, zss.at[c, q], zrs.at[c, q], at_z(sign)).wait_recv()
        return zr[c, q, 0:rows, :].astype(F32)

    def put_z(c, k, far, rows=ROWS):
        src, dst = zs.at[c, k, pl.ds(0, rows)], zr.at[c, k, pl.ds(0, rows)]
        send(src, dst, zss.at[c, k], zrs.at[c, k], at_z(far))

    def part(c, far):
        return pbuf.at[c, lax.rem(z + far + NZ, NZ)]

    def first(c):
        for d, sign in ((0, 1), (1, -1)):
            lo = 32 * d
            zs[c, 4 * d, 0:32, :] = part(c, 4)[lo:lo + 32, :].astype(BF)
            put_z(c, 4 * d, sign, 32)
            if c in TWO:
                zs[c, 4 * d + 1] = part(c, 2 * sign)[...].astype(BF)
                put_z(c, 4 * d + 1, sign)

    def with_half(c, k, d, sign):
        lo, other = 32 * d, 32 - 32 * d
        mine = part(c, 3 * sign)
        got = got_z(c, 4 * d, sign, 32)
        zs[c, k, lo:lo + 32, :] = (mine[lo:lo + 32, :] + got).astype(BF)
        zs[c, k, other:other + 32, :] = mine[other:other + 32, :].astype(BF)

    def hop(c, s, d):
        sign = 1 - 2 * d
        k = d * 4 + s - 1
        if s == 2:
            with_half(c, k, d, sign)
        else:
            zs[c, k] = (part(c, sign * (5 - s))[...] + got_z(c, k - 1, sign)).astype(BF)
        put_z(c, k, sign)

    def pair(c, d):
        sign = 1 - 2 * d
        with_half(c, 4 * d + 2, d, sign)
        put_z(c, 4 * d + 2, 3 * sign)
        zs[c, 4 * d + 3] = (part(c, sign)[...] + got_z(c, 4 * d + 1, sign)).astype(BF)
        put_z(c, 4 * d + 3, sign)

    lane = lax.broadcasted_iota(jnp.int32, (8, 128), 1)

    def of_block(b, table):
        return jnp.where(lane < ROWS, table(0, b // 2), table(1, b // 2))

    def class_or_none(m, s):
        return jnp.where(s < live_ref[0, m], cls_ref[0, m, s], -1)

    def alive(m, s):
        return jnp.where(s < live_ref[0, m], 1, 0)

    def emit(c):
        b, m = rows_of(ORDER[c])
        fin[c] = pbuf[c, z].astype(BF)
        send(
            fin.at[c], out_ref.at[m, pl.ds(pl.multiple_of(b * ROWS, ROWS), ROWS)],
            fs.at[c], fr.at[c], before,
        )

    adapters_in = [False]

    def finish(c):
        total = pbuf[c, z]
        for q in (2, 3, 6, 7) if c in TWO else (3, 7):
            total = total + got_z(c, q, 1)
        b, m = rows_of(ORDER[c])
        keep = jnp.zeros((ROWS, 128), jnp.int32) + alive(m, b // 2)
        total = jnp.where(keep > 0, total, 0.0)
        if adapters_in[0]:
            total = total + lt[c]
        pbuf[c, z] = total
        if adapters_in[0]:
            emit(c)

    def up_relay():
        remote(uy, uy, uss.at[0], urs.at[0], at_y).wait_recv()
        for j in range(1, NX):
            there = lax.rem(x + j, NX)
            send(uy.at[there // 2], ug.at[hp], uss.at[3 + j], urs.at[3 + j], at_x(j))
        ug[hp] = uy[x // 2]

    def up_rows():
        for j in range(1, NX):
            for k, src in zip((j, 3 + j), from_x(j)):
                remote(ug.at[src], ug.at[src], uss.at[k], urs.at[k], at_x(j)).wait_recv()
        own = jnp.concatenate([gall[0], gall[1]], 0)
        both = nt(ug[...].reshape(128, 1024), own).reshape(8, 2, 8, 128)
        keep = of_block(h, alive)[None] > 0
        half = jnp.where(lane[None] < ROWS, both[:, 0], both[:, 1])
        mine = jnp.where(keep, half, 0.0).reshape(64, 128).astype(BF)
        plb[...] = mine
        plr[z] = mine
        for j in (4, 3, 5, 2, 6, 1, 7):
            send(plb, plr.at[z], l1s.at[j], l1r.at[j], at_z(j))

    def rank_sum():
        for j in range(1, NZ):
            src = lax.rem(z - j + NZ, NZ)
            remote(plr.at[src], plr.at[src], l1s.at[j], l1r.at[j], at_z(j)).wait_recv()
        mine = jnp.sum(plr[...].astype(F32), 0).astype(BF)
        l3b[...] = mine
        lfull[h] = mine
        send(l3b, lfull.at[h], l3s.at[0], l3r.at[0], at_y)
        for j in range(1, NX):
            send(l3b, lfull.at[h], l3s.at[j], l3r.at[j], at_x(j))
        for j in range(1, NZ):
            src = lax.rem(z - j + NZ, NZ)
            remote(hz.at[src], hz.at[src], h1s.at[j], h1r.at[j], at_z(j)).wait_recv()
        hv = hz[...].astype(F32)
        hv = jnp.concatenate([hv[:, 0].reshape(64, 64), hv[:, 1].reshape(64, 64)], 0).astype(BF)
        r = lax.broadcasted_iota(jnp.int32, (64, 64), 0)
        c = lax.broadcasted_iota(jnp.int32, (64, 64), 1)
        hkb[...] = nt(jnp.where(r == c, 1.0, 0.0).astype(BF), hv).reshape(8, 8, 128)
        hk[h] = hkb[h]
        send(hkb.at[pl.ds(NX * (1 - yh), NX)], hy, h2s.at[0], h2r.at[0], at_y)
        for j in range(1, NX):
            there = yh * NX + lax.rem(x + j, NX)
            send(hkb.at[there], hk.at[h], h2s.at[j], h2r.at[j], at_x(j))

    def rank_relay():
        remote(lfull.at[hp], lfull.at[hp], l3s.at[0], l3r.at[0], at_y).wait_recv()
        for j in range(1, NX):
            send(lfull.at[hp], lfull.at[hp], l3s.at[3 + j], l3r.at[3 + j], at_x(j))
        remote(hy, hy, h2s.at[0], h2r.at[0], at_y).wait_recv()
        for j in range(1, NX):
            there = lax.rem(x + j, NX)
            send(hy.at[there], hk.at[hp], h2s.at[3 + j], h2r.at[3 + j], at_x(j))
        hk[hp] = hy[x]

    def rank_here(done):
        for j in range(1, NX):
            for k, src in zip((j, 3 + j), from_x(j)):
                remote(lfull.at[src], lfull.at[src], l3s.at[k], l3r.at[k], at_x(j)).wait_recv()
        loads[4].wait()
        r = lax.broadcasted_iota(jnp.int32, (128, 128), 0)
        c = lax.broadcasted_iota(jnp.int32, (128, 128), 1)
        eye = jnp.where(r == c, 1.0, 0.0).astype(BF)
        for name in ("O", "L", "R", "X", "Y", "YL", "YR", "YX"):
            b, _ = rows_of(name + "0")
            turned = nt(eye, lfull[b]).astype(BF)
            for m in range(2):
                slot = SLOT[name + str(m)]
                term = nn(turned[m * ROWS:(m + 1) * ROWS], av[cls_ref[0, m, b // 2]])
                if slot in done:
                    pbuf[slot, z] = pbuf[slot, z] + term
                else:
                    lt[slot] = term
        adapters_in[0] = True
        for slot in done:
            emit(slot)

    def up_gradient():
        for j in range(1, NX):
            for k, src in zip((j, 3 + j), from_x(j)):
                remote(hk.at[src], hk.at[src], h2s.at[k], h2r.at[k], at_x(j)).wait_recv()
        number = lax.broadcasted_iota(jnp.int32, (8, 8, 128), 0)
        left, right = [], []
        for name in ("O", "L", "R", "X", "Y", "YL", "YR", "YX"):
            b, _ = rows_of(name + "0")
            chosen = of_block(b, class_or_none)[None]
            left.append(jnp.where(number == chosen, hk[b][None], 0.0).reshape(64, 128).astype(BF))
            right.append(gall[SLOT[name + "0"]])
            right.append(gall[SLOT[name + "1"]])
        du_ref[...] = nn(jnp.concatenate(left, 1), jnp.concatenate(right, 0)).astype(BF)

    def down_gradient():
        loads[3].wait()
        number = lax.broadcasted_iota(jnp.int32, (8, 64, 128), 0)
        for b in range(NH):
            wide = lax.broadcasted_iota(jnp.int32, (64, 128), 1)
            chosen = jnp.where(wide < ROWS, class_or_none(0, b // 2), class_or_none(1, b // 2))[None]
            left = jnp.where(number == chosen, lfull[b].astype(F32)[None], 0.0)
            left = left.reshape(512, 128).astype(BF)
            right = jnp.concatenate(
                [xv[0, b * ROWS:(b + 1) * ROWS], xv[1, b * ROWS:(b + 1) * ROWS]], 0
            )
            term = nn(left, right)
            if b == 0:
                dacc[...] = term
            elif b < NH - 1:
                dacc[...] += term
            else:
                da_ref[...] = (dacc[...] + term).astype(BF)

    done = []

    def multiply(*chunks):
        for c in chunks:
            arrive(ORDER[c])
        prod = nn(jnp.concatenate([gall[c] for c in chunks], 0), wt[...])
        for i, c in enumerate(chunks):
            for j in range(NZ):
                pbuf[c, j] = prod[i * ROWS:(i + 1) * ROWS, j * 128:(j + 1) * 128]
            first(c)

    def close(c):
        finish(c)
        if not adapters_in[0]:
            done.append(c)

    does = {
        "fwd": lambda name, half: arrive(name, (half,)),
        "mm": multiply, "hop": hop, "pair": pair, "fin": close,
        "up_relay": up_relay, "up_rows": up_rows, "rank_sum": rank_sum,
        "rank_relay": rank_relay, "rank_here": lambda: rank_here(tuple(done)),
        "up_gradient": up_gradient, "down_gradient": down_gradient,
    }
    for what, *which in PLAN:
        does[what](*which)

    for c in range(N):
        b, m = rows_of(ORDER[c])
        dst = out_ref.at[m, pl.ds(pl.multiple_of(b * ROWS, ROWS), ROWS)]
        remote(fin.at[c], dst, fs.at[c], fr.at[c], before).wait_recv()
    for copy in sends:
        copy.wait_send()


def hand_out(out, da, du, out_to, da_to, du_to):
    out_to[...] = out[...]
    da_to[...] = da[...]
    du_to[...] = du[...]


def shards(
    output_gradient, forward_input, saved_rank_outputs, projection_weight,
    adapter_down_maps, adapter_up_maps, segment_adapter_class, live_segment_table,
):
    vm = pltpu.VMEM
    dma = pltpu.SemaphoreType.DMA
    vmem = pl.BlockSpec(memory_space=pltpu.VMEM)
    hbm = pl.BlockSpec(memory_space=pl.ANY)
    shapes = (
        jax.ShapeDtypeStruct((2, 512, 128), BF),
        jax.ShapeDtypeStruct((512, 128), BF),
        jax.ShapeDtypeStruct((64, 1024), BF),
    )
    outs = pl.pallas_call(
        section,
        name="section",
        out_shape=shapes,
        in_specs=[hbm, hbm, hbm, hbm, hbm, hbm, hbm, hbm],
        out_specs=(vmem, vmem, vmem),
        scratch_shapes=[
            vm((N, ROWS, 1024), BF), vm((1024, 1024), BF), vm((1024, 1024), BF), vm((N, 8, ROWS, 128), F32),
            vm((N, 8, ROWS, 128), BF), vm((N, 8, ROWS, 128), BF),
            vm((8, 8, 1024), F32), vm((4, 16, 1024), BF), vm((8, 16, 1024), BF),
            vm((64, 128), BF), vm((8, 64, 128), BF), vm((64, 128), BF), vm((8, 64, 128), BF),
            vm((N, ROWS, 128), F32),
            vm((8, 2, 8, 64), BF), vm((8, 8, 128), F32), vm((8, 8, 128), F32),
            vm((2, 512, 128), BF), vm((8, 64, 128), BF), vm((N, ROWS, 128), BF), vm((512, 128), F32),
            vm((64, 1024), BF), vm((2, 8, 64), BF),
            vm((2, 16, 1024), BF), vm((4, 8, 128), F32),
            pltpu.SMEM((1, 2, 4), jnp.int32), pltpu.SMEM((1, 2), jnp.int32),
            dma((9,)), dma((32,)), dma((N, 2)), dma((N, 8)), dma((N, 8)),
            dma((8,)), dma((8,)), dma((8,)), dma((8,)), dma((8,)), dma((8,)),
            dma((8,)), dma((8,)), dma((8,)), dma((8,)), dma((N,)), dma((N,)),
        ],
        compiler_params=pltpu.CompilerParams(
            collective_id=0, has_side_effects=True, vmem_limit_bytes=40 * 1024 * 1024
        ),
    )(
        pltpu.with_memory_space_constraint(segment_adapter_class, pltpu.HBM),
        pltpu.with_memory_space_constraint(live_segment_table, pltpu.HBM),
        pltpu.with_memory_space_constraint(output_gradient.reshape(2, ROWS, 1024), pltpu.HBM),
        pltpu.with_memory_space_constraint(forward_input.reshape(2, 512, 128), pltpu.HBM),
        pltpu.with_memory_space_constraint(saved_rank_outputs.reshape(2, 8, 64), pltpu.HBM),
        pltpu.with_memory_space_constraint(projection_weight.reshape(1024, 1024), pltpu.HBM),
        pltpu.with_memory_space_constraint(adapter_down_maps.reshape(8, 64, 128), pltpu.HBM),
        pltpu.with_memory_space_constraint(adapter_up_maps.reshape(64, 1024), pltpu.HBM),
    )
    out, da, du = pl.pallas_call(
        hand_out,
        name="hand_out",
        out_shape=shapes,
        in_specs=[vmem] * 3,
        out_specs=(vmem,) * 3,
    )(*[pltpu.with_memory_space_constraint(o, pltpu.VMEM) for o in outs])
    return (
        out.reshape(1, 2, 512, 128),
        da.reshape(1, 8, 64, 128),
        du.reshape(1, 1, 8, 8, 1024),
    )


def solution(mesh):
    in_specs = (
        P("pipe", "tensor", None, None, None),
        P("pipe", None, None, "tensor"),
        P("pipe", None, "tensor", None),
        P("pipe", "tensor", None, None),
        P("pipe", None, None, "tensor"),
        P("pipe", "tensor", None, None, None),
        P("pipe", None, None),
        P("pipe", None),
    )
    out_specs = (
        P("pipe", None, None, "tensor"),
        P("pipe", None, None, "tensor"),
        P("pipe", "tensor", None, None, None),
    )
    return jax.shard_map(shards, mesh=mesh, in_specs=in_specs, out_specs=out_specs, check_vma=False)
```

```python
import jax
import jax.numpy as jnp
from jax import lax
from jax.experimental import pallas as pl
from jax.experimental.pallas import tpu as pltpu
from jax.sharding import PartitionSpec as P

MESH = pl.DeviceIdType.MESH
BF = jnp.bfloat16
F32 = jnp.float32
NX, NZ, NH, NP = 4, 8, 8, 8
ROWS = 64
ORDER = (
    "O0", "O1", "L0", "R0", "L1", "R1", "X0", "X1",
    "Y0", "YL0", "YR0", "Y1", "YX0", "YL1", "YR1", "YX1",
)
SLOT = {name: i for i, name in enumerate(ORDER)}
N = len(ORDER)
TWO = (7, 13, 14, 15)
SHIFT = {"O": 0, "L": 3, "R": 1, "X": 2, "Y": 0, "YL": 3, "YR": 1, "YX": 2}
ONWARD = {
    ("L0", 0): ((1, "X0"),),
    ("L1", 0): ((1, "X1"),),
    ("R0", 1): ((-1, "X0"),),
    ("R1", 1): ((-1, "X1"),),
    ("Y0", 0): ((1, "YL0"), (-1, "YR0")),
    ("Y0", 1): ((1, "YL0"), (-1, "YR0"), (2, "YX0")),
    ("Y1", 0): ((1, "YL1"), (-1, "YR1")),
    ("Y1", 1): ((1, "YL1"), (-1, "YR1"), (2, "YX1")),
    ("YL0", 0): ((1, "YX0"),),
    ("YL1", 0): ((1, "YX1"),),
}
PLAN = (
    ("mm", 0, 1), ("hop", 0, 2, 0), ("hop", 0, 2, 1), ("hop", 1, 2, 1), ("hop", 1, 2, 0), ("fwd", "L0", 0),
    ("fwd", "R0", 1), ("mm", 2, 3), ("hop", 0, 3, 0), ("hop", 0, 3, 1), ("fwd", "L1", 0), ("hop", 1, 3, 0),
    ("hop", 1, 3, 1), ("up_relay",), ("fwd", "R1", 1), ("mm", 4, 5), ("hop", 2, 2, 0), ("hop", 2, 2, 1),
    ("hop", 3, 2, 1), ("hop", 3, 2, 0), ("hop", 0, 4, 0), ("hop", 0, 4, 1), ("hop", 1, 4, 0),
    ("hop", 1, 4, 1), ("fwd", "Y0", 0), ("mm", 6), ("hop", 4, 2, 0), ("hop", 5, 2, 0), ("hop", 2, 3, 0),
    ("hop", 5, 2, 1), ("hop", 2, 3, 1), ("hop", 3, 3, 0), ("hop", 3, 3, 1), ("hop", 4, 2, 1),
    ("fwd", "Y0", 1), ("mm", 8), ("fin", 1), ("fin", 0), ("up_rows",), ("fwd", "YL0", 0), ("hop", 6, 2, 0),
    ("hop", 6, 2, 1), ("hop", 4, 3, 0), ("hop", 5, 3, 1), ("hop", 5, 3, 0), ("fwd", "Y1", 0), ("mm", 7),
    ("hop", 2, 4, 1), ("hop", 8, 2, 0), ("hop", 4, 3, 1), ("hop", 3, 4, 0), ("hop", 2, 4, 0),
    ("hop", 3, 4, 1), ("hop", 8, 2, 1), ("mm", 9, 10), ("fwd", "Y1", 1), ("mm", 11), ("mm", 12),
    ("hop", 6, 3, 0), ("hop", 5, 4, 1), ("hop", 4, 4, 0), ("hop", 6, 3, 1), ("hop", 5, 4, 0), ("pair", 7, 1),
    ("fwd", "YL1", 0), ("pair", 7, 0), ("hop", 8, 3, 0), ("hop", 4, 4, 1), ("rank_sum",), ("fin", 2),
    ("hop", 9, 2, 0), ("hop", 10, 2, 1), ("hop", 10, 2, 0), ("hop", 9, 2, 1), ("hop", 8, 3, 1),
    ("hop", 12, 2, 0), ("hop", 12, 2, 1), ("hop", 11, 2, 0), ("hop", 6, 4, 0), ("hop", 11, 2, 1),
    ("mm", 13, 14), ("hop", 6, 4, 1), ("fin", 5), ("fin", 3), ("mm", 15), ("hop", 8, 4, 0), ("hop", 10, 3, 1),
    ("fin", 4), ("hop", 9, 3, 1), ("hop", 9, 3, 0), ("hop", 10, 3, 0), ("hop", 8, 4, 1), ("hop", 12, 3, 0),
    ("hop", 12, 3, 1), ("fin", 7), ("hop", 11, 3, 0), ("hop", 11, 3, 1), ("rank_relay",), ("pair", 13, 1),
    ("pair", 13, 0), ("pair", 14, 1), ("pair", 14, 0), ("fin", 6), ("pair", 15, 0), ("pair", 15, 1),
    ("hop", 10, 4, 1), ("hop", 9, 4, 0), ("hop", 9, 4, 1), ("hop", 10, 4, 0), ("fin", 8), ("hop", 12, 4, 0),
    ("hop", 12, 4, 1), ("hop", 11, 4, 0), ("hop", 11, 4, 1), ("rank_here",), ("fin", 13), ("fin", 14),
    ("fin", 9), ("fin", 10), ("fin", 12), ("fin", 15), ("fin", 11), ("up_gradient",), ("down_gradient",),
)


def nt(a, b):
    return lax.dot_general(a, b, (((1,), (1,)), ((), ())), preferred_element_type=F32)


def nn(a, b):
    return lax.dot_general(a, b, (((1,), (0,)), ((), ())), preferred_element_type=F32)


def section(
    cls_at, live_at, g_ref, x_ref, hid_ref, w_ref, a_ref, u_ref,
    out_ref, da_ref, du_ref,
    gall, wv, wt, pbuf, zs, zr, uf, us, ug, plb, plr, l3b, lfull, lt,
    hz, hkb, hk, xv, av, fin, dacc, uv, hidv, uy, hy, cls_ref, live_ref,
    loc, gss, grs, zss, zrs, uss, urs, l1s, l1r, l3s, l3r, h1s, h1r, h2s, h2r, fs, fr,
):
    p = lax.axis_index("pipe")
    t = lax.axis_index("tensor")
    z = lax.rem(t, NZ)
    h = t // NZ
    x = lax.rem(h, NX)
    yh = h // NX

    def at_z(j):
        return (p, h * NZ + lax.rem(z + j + NZ, NZ))

    def at_x(j):
        return (p, (yh * NX + lax.rem(x + j + NX, NX)) * NZ + z)

    hp = (1 - yh) * NX + x
    at_y = (p, hp * NZ + z)

    def from_x(j):
        return yh * NX + lax.rem(x - j + NX, NX), (1 - yh) * NX + lax.rem(x - j + NX, NX)

    before = (lax.rem(p + NP - 1, NP), t)
    after = (lax.rem(p + 1, NP), t)

    def rows_of(name):
        shift = SHIFT[name[:-1]]
        there = 1 - yh if name[0] == "Y" else yh
        return there * NX + lax.rem(x + shift, NX), int(name[-1])

    bar = pltpu.get_barrier_semaphore()
    for j in range(1, NZ):
        pl.semaphore_signal(bar, inc=1, device_id=at_z(j), device_id_type=MESH)
    for j in range(1, NX):
        pl.semaphore_signal(bar, inc=1, device_id=at_x(j), device_id_type=MESH)
    pl.semaphore_signal(bar, inc=1, device_id=at_y, device_id_type=MESH)
    pl.semaphore_signal(bar, inc=1, device_id=before, device_id_type=MESH)
    pl.semaphore_signal(bar, inc=1, device_id=after, device_id_type=MESH)

    loads = [
        pltpu.make_async_copy(cls_at, cls_ref, loc.at[7]),
        pltpu.make_async_copy(live_at, live_ref, loc.at[8]),
        pltpu.make_async_copy(u_ref, uv, loc.at[5]),
        pltpu.make_async_copy(hid_ref, hidv, loc.at[6]),
        pltpu.make_async_copy(g_ref.at[0], gall.at[0], loc.at[0]),
        pltpu.make_async_copy(g_ref.at[1], gall.at[1], loc.at[1]),
        pltpu.make_async_copy(w_ref, wv, loc.at[2]),
        pltpu.make_async_copy(x_ref, xv, loc.at[3]),
        pltpu.make_async_copy(a_ref, av, loc.at[4]),
    ]
    for load in loads:
        load.start()
    for _ in range(4):
        loads.pop(0).wait()

    uf[...] = uv[...].astype(F32).reshape(uf.shape)
    for s in range(4):
        us[s] = jnp.concatenate([uf[cls_ref[0, 0, s]], uf[cls_ref[0, 1, s]]], 0).astype(BF)
    ug[h] = us[h // 2]
    hz[z] = hidv[...]

    pl.semaphore_wait(bar, 13)

    sends = []

    def remote(src, dst, ssem, rsem, where):
        return pltpu.make_async_remote_copy(
            src_ref=src, dst_ref=dst, send_sem=ssem, recv_sem=rsem,
            device_id=where, device_id_type=MESH,
        )

    def send(*args):
        copy = remote(*args)
        copy.start()
        sends.append(copy)

    count = [0]

    def g_send(src, where, name, half):
        slot = SLOT[name]
        dst = gall.at[slot, pl.ds(32 * half, 32)]
        send(src, dst, gss.at[count[0]], grs.at[slot, half], where)
        count[0] += 1

    def own(m, half):
        return g_ref.at[m, pl.ds(32 * half, 32)]

    send(us.at[pl.ds(2 * (1 - yh), 2)], uy, uss.at[0], urs.at[0], at_y)
    for m in range(2):
        for half in range(2):
            g_send(own(m, half), at_x(1), f"L{m}", half)
            g_send(own(m, half), at_x(-1), f"R{m}", half)
            g_send(own(m, half), at_y, f"Y{m}", half)
    for j in range(1, NZ):
        send(hidv, hz.at[z], h1s.at[j], h1r.at[j], at_z(j))
    for j in range(1, NX):
        there = lax.rem(x + j, NX)
        send(us.at[2 * yh + there // 2], ug.at[h], uss.at[j], urs.at[j], at_x(j))
    here = set()

    def arrive(name, halves=(0, 1)):
        slot = SLOT[name]
        for half in halves:
            if (name, half) in here:
                continue
            here.add((name, half))
            got = gall.at[slot, pl.ds(32 * half, 32)]
            if slot < 2:
                if half == 0:
                    loads[slot].wait()
            else:
                remote(got, got, gss.at[0], grs.at[slot, half], at_y).wait_recv()
            for direction, name_there in ONWARD.get((name, half), ()):
                g_send(got, at_x(direction), name_there, half)

    def got_z(c, q, sign, rows=ROWS):
        got = zr.at[c, q, pl.ds(0, rows)]
        remote(got, got, zss.at[c, q], zrs.at[c, q], at_z(sign)).wait_recv()
        return zr[c, q, 0:rows, :].astype(F32)

    def put_z(c, k, far, rows=ROWS):
        src, dst = zs.at[c, k, pl.ds(0, rows)], zr.at[c, k, pl.ds(0, rows)]
        send(src, dst, zss.at[c, k], zrs.at[c, k], at_z(far))

    def part(c, far):
        return pbuf.at[c, lax.rem(z + far + NZ, NZ)]

    def first(c):
        for d, sign in ((0, 1), (1, -1)):
            lo = 32 * d
            zs[c, 4 * d, 0:32, :] = part(c, 4)[lo:lo + 32, :].astype(BF)
            put_z(c, 4 * d, sign, 32)
            if c in TWO:
                zs[c, 4 * d + 1] = part(c, 2 * sign)[...].astype(BF)
                put_z(c, 4 * d + 1, sign)

    def with_half(c, k, d, sign):
        lo, other = 32 * d, 32 - 32 * d
        mine = part(c, 3 * sign)
        got = got_z(c, 4 * d, sign, 32)
        zs[c, k, lo:lo + 32, :] = (mine[lo:lo + 32, :] + got).astype(BF)
        zs[c, k, other:other + 32, :] = mine[other:other + 32, :].astype(BF)

    def hop(c, s, d):
        sign = 1 - 2 * d
        k = d * 4 + s - 1
        if s == 2:
            with_half(c, k, d, sign)
        else:
            zs[c, k] = (part(c, sign * (5 - s))[...] + got_z(c, k - 1, sign)).astype(BF)
        put_z(c, k, sign)

    def pair(c, d):
        sign = 1 - 2 * d
        with_half(c, 4 * d + 2, d, sign)
        put_z(c, 4 * d + 2, 3 * sign)
        zs[c, 4 * d + 3] = (part(c, sign)[...] + got_z(c, 4 * d + 1, sign)).astype(BF)
        put_z(c, 4 * d + 3, sign)

    lane = lax.broadcasted_iota(jnp.int32, (8, 128), 1)

    def of_block(b, table):
        return jnp.where(lane < ROWS, table(0, b // 2), table(1, b // 2))

    def class_or_none(m, s):
        return jnp.where(s < live_ref[0, m], cls_ref[0, m, s], -1)

    def alive(m, s):
        return jnp.where(s < live_ref[0, m], 1, 0)

    def emit(c):
        b, m = rows_of(ORDER[c])
        fin[c] = pbuf[c, z].astype(BF)
        send(
            fin.at[c], out_ref.at[m, pl.ds(pl.multiple_of(b * ROWS, ROWS), ROWS)],
            fs.at[c], fr.at[c], before,
        )

    adapters_in = [False]

    def finish(c):
        total = pbuf[c, z]
        for q in (2, 3, 6, 7) if c in TWO else (3, 7):
            total = total + got_z(c, q, 1)
        b, m = rows_of(ORDER[c])
        keep = jnp.zeros((ROWS, 128), jnp.int32) + alive(m, b // 2)
        total = jnp.where(keep > 0, total, 0.0)
        if adapters_in[0]:
            total = total + lt[c]
        pbuf[c, z] = total
        if adapters_in[0]:
            emit(c)

    def up_relay():
        remote(uy, uy, uss.at[0], urs.at[0], at_y).wait_recv()
        for j in range(1, NX):
            there = lax.rem(x + j, NX)
            send(uy.at[there // 2], ug.at[hp], uss.at[3 + j], urs.at[3 + j], at_x(j))
        ug[hp] = uy[x // 2]

    def up_rows():
        for j in range(1, NX):
            for k, src in zip((j, 3 + j), from_x(j)):
                remote(ug.at[src], ug.at[src], uss.at[k], urs.at[k], at_x(j)).wait_recv()
        own = jnp.concatenate([gall[0], gall[1]], 0)
        both = nt(ug[...].reshape(128, 1024), own).reshape(8, 2, 8, 128)
        keep = of_block(h, alive)[None] > 0
        half = jnp.where(lane[None] < ROWS, both[:, 0], both[:, 1])
        mine = jnp.where(keep, half, 0.0).reshape(64, 128).astype(BF)
        plb[...] = mine
        plr[z] = mine
        for j in (4, 3, 5, 2, 6, 1, 7):
            send(plb, plr.at[z], l1s.at[j], l1r.at[j], at_z(j))

    def rank_sum():
        for j in range(1, NZ):
            src = lax.rem(z - j + NZ, NZ)
            remote(plr.at[src], plr.at[src], l1s.at[j], l1r.at[j], at_z(j)).wait_recv()
        mine = jnp.sum(plr[...].astype(F32), 0).astype(BF)
        l3b[...] = mine
        lfull[h] = mine
        send(l3b, lfull.at[h], l3s.at[0], l3r.at[0], at_y)
        for j in range(1, NX):
            send(l3b, lfull.at[h], l3s.at[j], l3r.at[j], at_x(j))
        for j in range(1, NZ):
            src = lax.rem(z - j + NZ, NZ)
            remote(hz.at[src], hz.at[src], h1s.at[j], h1r.at[j], at_z(j)).wait_recv()
        hv = hz[...].astype(F32)
        hv = jnp.concatenate([hv[:, 0].reshape(64, 64), hv[:, 1].reshape(64, 64)], 0).astype(BF)
        r = lax.broadcasted_iota(jnp.int32, (64, 64), 0)
        c = lax.broadcasted_iota(jnp.int32, (64, 64), 1)
        hkb[...] = nt(jnp.where(r == c, 1.0, 0.0).astype(BF), hv).reshape(8, 8, 128)
        hk[h] = hkb[h]
        send(hkb.at[pl.ds(NX * (1 - yh), NX)], hy, h2s.at[0], h2r.at[0], at_y)
        for j in range(1, NX):
            there = yh * NX + lax.rem(x + j, NX)
            send(hkb.at[there], hk.at[h], h2s.at[j], h2r.at[j], at_x(j))

    def rank_relay():
        remote(lfull.at[hp], lfull.at[hp], l3s.at[0], l3r.at[0], at_y).wait_recv()
        for j in range(1, NX):
            send(lfull.at[hp], lfull.at[hp], l3s.at[3 + j], l3r.at[3 + j], at_x(j))
        remote(hy, hy, h2s.at[0], h2r.at[0], at_y).wait_recv()
        for j in range(1, NX):
            there = lax.rem(x + j, NX)
            send(hy.at[there], hk.at[hp], h2s.at[3 + j], h2r.at[3 + j], at_x(j))
        hk[hp] = hy[x]

    def rank_here(done):
        for j in range(1, NX):
            for k, src in zip((j, 3 + j), from_x(j)):
                remote(lfull.at[src], lfull.at[src], l3s.at[k], l3r.at[k], at_x(j)).wait_recv()
        loads[4].wait()
        r = lax.broadcasted_iota(jnp.int32, (128, 128), 0)
        c = lax.broadcasted_iota(jnp.int32, (128, 128), 1)
        eye = jnp.where(r == c, 1.0, 0.0).astype(BF)
        for name in ("O", "L", "R", "X", "Y", "YL", "YR", "YX"):
            b, _ = rows_of(name + "0")
            turned = nt(eye, lfull[b]).astype(BF)
            for m in range(2):
                slot = SLOT[name + str(m)]
                term = nn(turned[m * ROWS:(m + 1) * ROWS], av[cls_ref[0, m, b // 2]])
                if slot in done:
                    pbuf[slot, z] = pbuf[slot, z] + term
                else:
                    lt[slot] = term
        adapters_in[0] = True
        for slot in done:
            emit(slot)

    def up_gradient():
        for j in range(1, NX):
            for k, src in zip((j, 3 + j), from_x(j)):
                remote(hk.at[src], hk.at[src], h2s.at[k], h2r.at[k], at_x(j)).wait_recv()
        number = lax.broadcasted_iota(jnp.int32, (8, 8, 128), 0)
        left, right = [], []
        for name in ("O", "L", "R", "X", "Y", "YL", "YR", "YX"):
            b, _ = rows_of(name + "0")
            chosen = of_block(b, class_or_none)[None]
            left.append(jnp.where(number == chosen, hk[b][None], 0.0).reshape(64, 128).astype(BF))
            right.append(gall[SLOT[name + "0"]])
            right.append(gall[SLOT[name + "1"]])
        du_ref[...] = nn(jnp.concatenate(left, 1), jnp.concatenate(right, 0)).astype(BF)

    def down_gradient():
        loads[3].wait()
        number = lax.broadcasted_iota(jnp.int32, (8, 64, 128), 0)
        for b in range(NH):
            wide = lax.broadcasted_iota(jnp.int32, (64, 128), 1)
            chosen = jnp.where(wide < ROWS, class_or_none(0, b // 2), class_or_none(1, b // 2))[None]
            left = jnp.where(number == chosen, lfull[b].astype(F32)[None], 0.0)
            left = left.reshape(512, 128).astype(BF)
            right = jnp.concatenate(
                [xv[0, b * ROWS:(b + 1) * ROWS], xv[1, b * ROWS:(b + 1) * ROWS]], 0
            )
            term = nn(left, right)
            if b == 0:
                dacc[...] = term
            elif b < NH - 1:
                dacc[...] += term
            else:
                da_ref[...] = (dacc[...] + term).astype(BF)

    loads[2].wait()
    wt[...] = wv[...].T
    done = []

    def multiply(*chunks):
        for c in chunks:
            arrive(ORDER[c])
        prod = nn(jnp.concatenate([gall[c] for c in chunks], 0), wt[...])
        for i, c in enumerate(chunks):
            for j in range(NZ):
                pbuf[c, j] = prod[i * ROWS:(i + 1) * ROWS, j * 128:(j + 1) * 128]
            first(c)

    def close(c):
        finish(c)
        if not adapters_in[0]:
            done.append(c)

    does = {
        "fwd": lambda name, half: arrive(name, (half,)),
        "mm": multiply, "hop": hop, "pair": pair, "fin": close,
        "up_relay": up_relay, "up_rows": up_rows, "rank_sum": rank_sum,
        "rank_relay": rank_relay, "rank_here": lambda: rank_here(tuple(done)),
        "up_gradient": up_gradient, "down_gradient": down_gradient,
    }
    for what, *which in PLAN:
        does[what](*which)

    for c in range(N):
        b, m = rows_of(ORDER[c])
        dst = out_ref.at[m, pl.ds(pl.multiple_of(b * ROWS, ROWS), ROWS)]
        remote(fin.at[c], dst, fs.at[c], fr.at[c], before).wait_recv()
    for copy in sends:
        copy.wait_send()


def hand_out(out, da, du, out_to, da_to, du_to):
    out_to[...] = out[...]
    da_to[...] = da[...]
    du_to[...] = du[...]


def shards(
    output_gradient, forward_input, saved_rank_outputs, projection_weight,
    adapter_down_maps, adapter_up_maps, segment_adapter_class, live_segment_table,
):
    vm = pltpu.VMEM
    dma = pltpu.SemaphoreType.DMA
    vmem = pl.BlockSpec(memory_space=pltpu.VMEM)
    hbm = pl.BlockSpec(memory_space=pl.ANY)
    shapes = (
        jax.ShapeDtypeStruct((2, 512, 128), BF),
        jax.ShapeDtypeStruct((512, 128), BF),
        jax.ShapeDtypeStruct((64, 1024), BF),
    )
    outs = pl.pallas_call(
        section,
        name="section",
        out_shape=shapes,
        in_specs=[hbm, hbm, hbm, hbm, hbm, hbm, hbm, hbm],
        out_specs=(vmem, vmem, vmem),
        scratch_shapes=[
            vm((N, ROWS, 1024), BF), vm((1024, 1024), BF), vm((1024, 1024), BF), vm((N, 8, ROWS, 128), F32),
            vm((N, 8, ROWS, 128), BF), vm((N, 8, ROWS, 128), BF),
            vm((8, 8, 1024), F32), vm((4, 16, 1024), BF), vm((8, 16, 1024), BF),
            vm((64, 128), BF), vm((8, 64, 128), BF), vm((64, 128), BF), vm((8, 64, 128), BF),
            vm((N, ROWS, 128), F32),
            vm((8, 2, 8, 64), BF), vm((8, 8, 128), F32), vm((8, 8, 128), F32),
            vm((2, 512, 128), BF), vm((8, 64, 128), BF), vm((N, ROWS, 128), BF), vm((512, 128), F32),
            vm((64, 1024), BF), vm((2, 8, 64), BF),
            vm((2, 16, 1024), BF), vm((4, 8, 128), F32),
            pltpu.SMEM((1, 2, 4), jnp.int32), pltpu.SMEM((1, 2), jnp.int32),
            dma((9,)), dma((32,)), dma((N, 2)), dma((N, 8)), dma((N, 8)),
            dma((8,)), dma((8,)), dma((8,)), dma((8,)), dma((8,)), dma((8,)),
            dma((8,)), dma((8,)), dma((8,)), dma((8,)), dma((N,)), dma((N,)),
        ],
        compiler_params=pltpu.CompilerParams(
            collective_id=0, has_side_effects=True, vmem_limit_bytes=40 * 1024 * 1024
        ),
    )(
        pltpu.with_memory_space_constraint(segment_adapter_class, pltpu.HBM),
        pltpu.with_memory_space_constraint(live_segment_table, pltpu.HBM),
        pltpu.with_memory_space_constraint(output_gradient.reshape(2, ROWS, 1024), pltpu.HBM),
        pltpu.with_memory_space_constraint(forward_input.reshape(2, 512, 128), pltpu.HBM),
        pltpu.with_memory_space_constraint(saved_rank_outputs.reshape(2, 8, 64), pltpu.HBM),
        pltpu.with_memory_space_constraint(projection_weight.reshape(1024, 1024), pltpu.HBM),
        pltpu.with_memory_space_constraint(adapter_down_maps.reshape(8, 64, 128), pltpu.HBM),
        pltpu.with_memory_space_constraint(adapter_up_maps.reshape(64, 1024), pltpu.HBM),
    )
    out, da, du = pl.pallas_call(
        hand_out,
        name="hand_out",
        out_shape=shapes,
        in_specs=[vmem] * 3,
        out_specs=(vmem,) * 3,
    )(*[pltpu.with_memory_space_constraint(o, pltpu.VMEM) for o in outs])
    return (
        out.reshape(1, 2, 512, 128),
        da.reshape(1, 8, 64, 128),
        du.reshape(1, 1, 8, 8, 1024),
    )


def solution(mesh):
    in_specs = (
        P("pipe", "tensor", None, None, None),
        P("pipe", None, None, "tensor"),
        P("pipe", None, "tensor", None),
        P("pipe", "tensor", None, None),
        P("pipe", None, None, "tensor"),
        P("pipe", "tensor", None, None, None),
        P("pipe", None, None),
        P("pipe", None),
    )
    out_specs = (
        P("pipe", None, None, "tensor"),
        P("pipe", None, None, "tensor"),
        P("pipe", "tensor", None, None, None),
    )
    return jax.shard_map(shards, mesh=mesh, in_specs=in_specs, out_specs=out_specs, check_vma=False)
```
